768 devices in a mesh: replica: 192 (over z_hi, y, x, core), fsdp: 4 (over z_lo).
Axes of the slice: x: 4, y: 8, z: 12 (z_hi: 3, z_lo: 4; z = z_hi * 4 + z_lo), core: 2. Of those that a mesh axis runs over, the one named last changes fastest.
Arguments:
- activations: bfloat16 [196608, 4096], P(('replica', 'fsdp')), may hold values from -6 to 6
- output_grads: bfloat16 [196608, 512], P(('replica', 'fsdp')), may hold values from -0.1875 to 0.1875
- momentum: bfloat16 [192, 4096, 512], P('replica', 'fsdp'), may hold values from -6 to 6
- chosen_blocks: int32 [192, 64, 8], P('replica', 'fsdp'), may hold values from 0 to 255, as said below
Outputs:
- momentum_next: bfloat16 [192, 4096, 512], P('replica', 'fsdp')
- update: float32 [4096, 512], P('fsdp')
The draws below stay inside these ranges and needn't reach their ends.
Inputs may be any that keep to these rules, and one draw needn't show every extreme that they name: `chosen_blocks`: the 8 numbers of each span row of each replica are different block numbers.
All inputs are finite; a program needn't handle non-finite values.
Results may differ from the reference program's by a relative error of at most 0.013.
Values may be sent and summed in bfloat16 or wider, within the bound.
A program may use at most 64 MiB of HBM per device.

```python
import jax
import jax.numpy as jnp
from jax import lax

DW = 4096
FW = 512
TOK_DEV = 256
SPAN = 64
BLOCK = 128
TOP = 8
REPLICAS = 192
TOKENS = 196608
CROWS = 64
BLOCKS = 256
N_FSDP = 4


def draw_chosen_blocks(key, part):
    scores = jax.random.randint(key, (REPLICAS, CROWS, BLOCKS), 0, 1 << 20, dtype=jnp.int32)
    scores = scores * BLOCKS + jnp.arange(BLOCKS, dtype=jnp.int32)[None, None, :]
    order = jnp.argsort(scores, axis=-1, stable=True)
    return order[:, :, :TOP].astype(jnp.int32)


def levels(key, shape, shards, smallest, high):
    factor_of, own = 1.0, jax.random.fold_in(key, 6)
    for dim, parts in shards:
        draws = jnp.exp(jax.random.uniform(jax.random.fold_in(own, dim), (parts,), jnp.float32, smallest / len(shards), high / len(shards)))
        factor_of = factor_of * jnp.repeat(draws, shape[dim] // parts).reshape([-1 if axis == dim else 1 for axis in range(len(shape))])
    return factor_of


def bell_draw(stream_key, dims, deviation, reach, pieces=(), held_as=jnp.bfloat16):
    drawn = deviation * jax.random.normal(stream_key, dims, jnp.float32)
    if pieces:
        drawn = drawn * levels(stream_key, dims, pieces, -0.22, 0.18)
    return jnp.clip(drawn, -reach, reach).astype(held_as)


def setup_inputs(seed: int = 0) -> dict:
    splits = jax.random.split(jax.random.key(seed), 5)
    return {
        "activations": bell_draw(splits[0], (TOKENS, DW), 1.0, 6.0, ((0, 768),)),
        "output_grads": bell_draw(splits[1], (TOKENS, FW), (0.5 / TOK_DEV ** 0.5), 0.1875, ((0, 768),)),
        "momentum": bell_draw(splits[2], (REPLICAS, DW, FW), 1.0, 6.0, ((0, 192), (1, 4))),
        "chosen_blocks": draw_chosen_blocks(jax.random.fold_in(splits[4], 71), 0),
    }


def cosine_table():
    order = jnp.arange(SPAN, dtype=jnp.float32)
    freq = order[:, None]
    place = order[None, :]
    factor = jnp.where(freq == 0.0, jnp.sqrt(jnp.float32(1.0 / SPAN)), jnp.sqrt(jnp.float32(2.0 / SPAN)))
    return factor * jnp.cos(jnp.float32(jnp.pi) * (2.0 * place + 1.0) * freq / (2.0 * SPAN))

def forward_blocks(field, table):
    rows = field.shape[0] // SPAN
    cols = field.shape[1] // SPAN
    shaped = field.reshape(rows, SPAN, cols, SPAN)
    coeffs = jnp.einsum('pu,cujv,qv->cjpq', table, shaped, table, precision=lax.Precision.HIGHEST)
    return coeffs.reshape(rows, cols * (SPAN * SPAN // BLOCK), BLOCK)

def inverse_blocks(coeffs, table):
    rows = coeffs.shape[0]
    cols = coeffs.shape[1] * BLOCK // (SPAN * SPAN)
    shaped = coeffs.reshape(rows, cols, SPAN, SPAN)
    field = jnp.einsum('pu,cjpq,qv->cujv', table, shaped, table, precision=lax.Precision.HIGHEST)
    return field.reshape(rows * SPAN, cols * SPAN)

def reference(activations, output_grads, momentum, chosen_blocks):
    table = cosine_table()
    xs = activations.reshape(REPLICAS, N_FSDP, TOK_DEV, DW)
    gs = output_grads.reshape(REPLICAS, N_FSDP, TOK_DEV, FW)
    numbers = jnp.arange(BLOCKS, dtype=jnp.int32)

    def one_replica(total, items):
        inputs, grads, moment_old, picks = items
        partial_terms = jnp.einsum('ftd,ftg->fdg', inputs.astype(jnp.float32), grads.astype(jnp.float32))
        rounded = lax.optimization_barrier(partial_terms.astype(jnp.bfloat16))
        grad = lax.optimization_barrier(jnp.sum(rounded.astype(jnp.float32), axis=0))
        moment = 0.9 * moment_old.astype(jnp.float32) + grad
        coeffs = forward_blocks(moment, table)
        mask = lax.optimization_barrier(jnp.sum((picks[:, :, None] == numbers[None, None, :]).astype(jnp.float32), axis=1))
        sent = lax.optimization_barrier((coeffs * mask[:, :, None]).astype(jnp.bfloat16))
        kept = coeffs * (1.0 - mask[:, :, None])
        moment_next = inverse_blocks(kept, table).astype(jnp.bfloat16)
        return (total + sent.astype(jnp.float32), moment_next)
    start = jnp.zeros((CROWS, BLOCKS, BLOCK), jnp.float32)
    total, momentum_next = lax.scan(one_replica, start, (xs, gs, momentum, chosen_blocks))
    update = inverse_blocks(total, table)
    return (momentum_next, update)
```

```python
import math

import jax
import jax.numpy as jnp
import numpy as np
from jax import lax
from jax.experimental import pallas as pl
from jax.experimental.pallas import tpu as pltpu
from jax.sharding import PartitionSpec as P

MESH = pl.DeviceIdType.MESH
F32 = jnp.float32
BF = jnp.bfloat16
SPAN = 64
NX, NY, NZ, NF = 8, 8, 3, 4
SLABS = 4


def tables():
    order = np.arange(SPAN)[:, None]
    place = np.arange(SPAN)[None, :]
    factor = np.where(order == 0, math.sqrt(1.0 / SPAN), math.sqrt(2.0 / SPAN))
    table = factor * np.cos(np.pi * (2 * place + 1) * order / (2 * SPAN))
    block = np.kron(np.eye(4), table).astype(np.float32)
    high = block.astype(jnp.bfloat16)
    low = (block - high.astype(np.float32)).astype(jnp.bfloat16)
    return high, low


def dot(a, b, ca=1, cb=0):
    return lax.dot_general(a, b, (((ca,), (cb,)), ((), ())), preferred_element_type=F32)


def split(a):
    high = a.astype(BF)
    return high, (a - high.astype(F32)).astype(BF)


def dot3(a, b, ca=1, cb=0):
    return dot(a[0], b[0], ca, cb) + dot(a[0], b[1], ca, cb) + dot(a[1], b[0], ca, cb)


def lanes_transform(value, table, cb):
    high, low = split(value)
    width = value.shape[1] // 256
    return jnp.concatenate(
        [
            dot3((high[:, 256 * t : 256 * t + 256], low[:, 256 * t : 256 * t + 256]), table, 1, cb)
            for t in range(width)
        ],
        axis=1,
    )


def iota(shape, dim):
    return lax.broadcasted_iota(jnp.int32, shape, dim)


def fold(value, span_col):
    lane = iota((value.shape[0], 128), 1)
    half = jnp.floor(span_col * 0.5)
    odd = span_col - 2.0 * half
    kept = jnp.zeros((value.shape[0], 128), F32)
    for s in range(4):
        kept = kept + jnp.where(half == float(s), value[:, 128 * s : 128 * s + 128], 0.0)
    kept = jnp.where((lane >> 6).astype(F32) == odd, kept, 0.0)
    return kept + pltpu.roll(kept, 64, 1)


def pack(rows):
    lane = iota((128, 128), 1)
    return jnp.where(lane < 64, rows[:128], rows[128:])


def kernel(
    x_hbm, g_hbm, mom_hbm, pk_ref, ch_ref, cl_ref, cth_ref, ctl_ref,
    out_m, out_u,
    xv, gv, mv, xr, gr, pk_all, csh, csl, jrow, trow, upart, usend, urecv,
    sent, a2, dp, by, zb, fin, mout,
    lsem, pk_s, pk_r, x_s, x_r, g_s, g_r, u_s, u_r, a_s, a_r, b_s, b_r,
    z_s, z_r, y_s, y_r, w_s, w_r, c_s, c_r,
):
    rep = lax.axis_index("replica")
    f = lax.axis_index("fsdp")
    m = lax.rem(rep, NX)
    row = rep - m
    y = lax.rem(lax.div(rep, NX), NY)
    zh = lax.div(rep, NX * NY)
    plane = lax.rem(rep, NX * NY)

    def line_peer(o):
        return (rep, lax.rem(f + o, NF))

    def row_peer(o):
        return (row + lax.rem(m + o, NX), f)

    def col_peer(o):
        return (zh * (NX * NY) + lax.rem(y + o, NY) * NX + m, f)

    def hi_peer(o):
        return (lax.rem(zh + o, NZ) * (NX * NY) + plane, f)

    loads = [
        pltpu.make_async_copy(x_hbm, xv, lsem.at[0]),
        pltpu.make_async_copy(g_hbm, gv, lsem.at[1]),
        pltpu.make_async_copy(mom_hbm, mv, lsem.at[2]),
    ]
    for copy in loads:
        copy.start()

    barrier = pltpu.get_barrier_semaphore()
    for make, count in ((line_peer, NF), (row_peer, NX), (col_peer, NY), (hi_peer, NZ)):
        for o in range(1, count):
            pl.semaphore_signal(barrier, inc=1, device_id=make(o), device_id_type=MESH)
    pl.semaphore_wait(barrier, NF + NX + NY + NZ - 4)

    sends = []

    def remote(src, dst, ssem, rsem, peer):
        copy = pltpu.make_async_remote_copy(
            src_ref=src, dst_ref=dst, send_sem=ssem, recv_sem=rsem,
            device_id=peer, device_id_type=MESH,
        )
        copy.start()
        sends.append(copy)
        return copy

    pk_copies = [
        remote(pk_ref, pk_all.at[f], pk_s.at[o - 1], pk_r.at[o - 1], line_peer(o))
        for o in range(1, NF)
    ]

    def send_x(slab):
        out = []
        for o in range(1, NF):
            peer = lax.rem(f + o, NF)
            cols = pl.ds(pl.multiple_of(peer * 1024 + slab * 256, 256), 256)
            k = slab * 3 + o - 1
            out.append(
                remote(
                    x_hbm.at[:, cols], xr.at[o - 1, :, pl.ds(slab * 256, 256)],
                    x_s.at[k], x_r.at[k], line_peer(o),
                )
            )
        return out

    x_copies = [send_x(0)]

    pk_all[f] = pk_ref[...]
    table = (ch_ref[...], cl_ref[...])
    loads[1].wait()
    gc = split(
        jnp.concatenate(
            [
                dot(gv[:, 256 * t : 256 * t + 256], table[0], 1, 1)
                + dot(gv[:, 256 * t : 256 * t + 256], table[1], 1, 1)
                for t in range(2)
            ],
            axis=1,
        )
    )
    for copy in pk_copies:
        copy.wait_recv()

    rows = iota((256, 128), 0)
    lane = iota((256, 128), 1)
    pick_lane = lane == ((rows >> 1) & 7)
    spread = (iota((256, 16), 1) == (iota((256, 16), 0) >> 4)).astype(BF)
    odd_row = (rows & 1).astype(F32)
    lane2 = iota((256, 256), 1).astype(F32)
    shift = (((iota((256, 1), 0) >> 4) & 3) * 64).astype(F32)
    loads[0].wait()
    for fi in range(NF):
        at = pl.ds(fi * 256, 256)
        number = jnp.sum(jnp.where(pick_lane, dot(spread, pk_all[fi]), 0.0), axis=1, keepdims=True)
        col = jnp.floor(number * (1.0 / 32.0))
        coeff_row = 2.0 * (number - 32.0 * col) + odd_row[:, :1]
        onehot = jnp.where(lane2 == coeff_row + shift, 1.0, 0.0).astype(BF)
        cs_high = dot(onehot, table[0]).astype(BF)
        cs_low = dot(onehot, table[1]).astype(BF)
        csh[at, :] = cs_high
        csl[at, :] = cs_low
        col_b = jnp.broadcast_to(col, (256, 128))
        jrow[at, :] = col_b
        trow[at, :] = jnp.broadcast_to(coeff_row + 64.0 * jnp.floor(col * 0.5), (256, 128))
        parts = []
        for s in range(SLABS):
            xs = xv[:, (fi * SLABS + s) * 256 : (fi * SLABS + s + 1) * 256]
            parts.append(
                dot(cs_high[64 * s : 64 * s + 64], xs, 1, 1)
                + dot(cs_low[64 * s : 64 * s + 64], xs, 1, 1)
            )
        value = dot3(split(jnp.concatenate(parts, axis=0)), gc)
        packed = pack(fold(value, col_b))
        upart[fi] = packed
        usend[fi] = packed.astype(BF)

    u_copies = [
        remote(
            usend.at[lax.rem(f + o, NF)], urecv.at[o - 1], u_s.at[o - 1], u_r.at[o - 1], line_peer(o)
        )
        for o in range(1, NF)
    ]
    x_copies.append(send_x(1))

    own = pl.multiple_of(f * 256, 256)
    loads[2].wait()
    parts = []
    for s in range(SLABS):
        high = csh[pl.ds(own + 64 * s, 64), :]
        low = csl[pl.ds(own + 64 * s, 64), :]
        ms = mv[256 * s : 256 * s + 256, :]
        parts.append(dot(high, ms) + dot(low, ms))
    col_b = jrow[pl.ds(own, 256), :]
    from_momentum = fold(lanes_transform(jnp.concatenate(parts, axis=0), table, 1), col_b)
    packed = upart[f] + 0.9 * pack(from_momentum)
    for copy in u_copies:
        copy.wait_recv()
    for o in range(3):
        packed = packed + urecv[o].astype(F32)
    packed = jnp.concatenate([packed, pltpu.roll(packed, 64, 1)], axis=0)
    col_odd = col_b - 2.0 * jnp.floor(col_b * 0.5)
    tile = jnp.where(lane < 64, packed, jnp.where(lane < 96, trow[pl.ds(own, 256), :], col_odd))
    sent[...] = tile.astype(BF)

    a_copies = []
    for o in range(1, NX):
        there = pl.ds(pl.multiple_of(lax.rem(m + o, NX) * 32, 32), 32)
        a_copies.append(
            remote(sent.at[there, :], a2.at[o - 1], a_s.at[o - 1], a_r.at[o - 1], row_peer(o))
        )
    a2[NX - 1] = sent[pl.ds(pl.multiple_of(m * 32, 32), 32), :]
    for copy in a_copies:
        copy.wait_recv()
    lane1 = iota((128, 128), 1)
    lane256 = iota((128, 256), 1).astype(F32)
    for u in range(2):
        got = jnp.concatenate(
            [a2[o, 16 * u : 16 * u + 16, :] for o in range(NX)], axis=0
        ).astype(F32)
        value = jnp.where(lane1 < 64, got, 0.0)
        value = value + pltpu.roll(value, 64, 1)
        value = jnp.where((lane1 >> 6).astype(F32) == got[:, 96:97], value, 0.0)
        onehot = jnp.where(lane256 == got[:, 64:65], 1.0, 0.0)
        dense = dot(onehot.astype(BF), value.astype(BF), 0, 0).astype(BF)
        for s in range(4):
            dp[4 * u + s] = dense[64 * s : 64 * s + 64]
    b_copies = [
        remote(
            dp.at[lax.rem(y + o, NY)], by.at[o - 1], b_s.at[o - 1], b_r.at[o - 1], col_peer(o)
        )
        for o in range(1, NY)
    ]
    plane_sum = dp[y].astype(F32)
    for copy in b_copies:
        copy.wait_recv()
    for o in range(NY - 1):
        plane_sum = plane_sum + by[o].astype(F32)
    zb[zh] = plane_sum.astype(BF)
    z_copies = [
        remote(zb.at[zh], zb.at[zh], z_s.at[o - 1], z_r.at[o - 1], hi_peer(o))
        for o in range(1, NZ)
    ]
    x_copies.append(send_x(2))
    x_copies.append(send_x(3))
    g_copies = [
        remote(g_hbm, gr.at[o - 1], g_s.at[o - 1], g_r.at[o - 1], line_peer(o))
        for o in range(1, NF)
    ]
    for copy in z_copies:
        copy.wait_recv()
    total = zb[0].astype(F32) + zb[1].astype(F32) + zb[2].astype(F32)
    left = dot3((cth_ref[:64, :64], ctl_ref[:64, :64]), split(total))
    piece = dot3(split(left), (ch_ref[:128, :128], cl_ref[:128, :128]))
    piece_rows = pl.ds(pl.multiple_of(m * 128 + lax.div(y, 4) * 64, 64), 64)
    piece_cols = pl.ds(pl.multiple_of(lax.rem(y, 4) * 128, 128), 128)
    fin[piece_rows, piece_cols] = piece.astype(BF)
    y_copies = [
        remote(
            fin.at[piece_rows, piece_cols], fin.at[piece_rows, piece_cols],
            y_s.at[o - 1], y_r.at[o - 1], col_peer(o),
        )
        for o in range(1, NY)
    ]
    for copy in y_copies:
        copy.wait_recv()
    band = pl.ds(pl.multiple_of(m * 128, 128), 128)
    w_copies = [
        remote(fin.at[band, :], fin.at[band, :], w_s.at[o - 1], w_r.at[o - 1], row_peer(2 * o))
        for o in range(1, 4)
    ]
    other = (row + m + 1 - 2 * lax.rem(m, 2), f)
    c_copies = [remote(fin.at[band, :], fin.at[band, :], c_s.at[0], c_r.at[0], other)]
    for o in range(1, 4):
        w_copies[o - 1].wait_recv()
        there = pl.ds(pl.multiple_of(lax.rem(m + NX - 2 * o, NX) * 128, 128), 128)
        c_copies.append(remote(fin.at[there, :], fin.at[there, :], c_s.at[o], c_r.at[o], other))
    for copy in c_copies:
        copy.wait_recv()
    u_out = pltpu.make_async_copy(fin, out_u, lsem.at[0])
    u_out.start()

    for copy in g_copies:
        copy.wait_recv()
    m_out = []
    lane512 = (iota((64, 512), 1) >> 6).astype(F32)
    for s in range(SLABS):
        for copy in x_copies[s]:
            copy.wait_recv()
        cols = pl.ds(pl.multiple_of(f * 1024 + s * 256, 256), 256)
        moment = 0.9 * mv[256 * s : 256 * s + 256, :].astype(F32)
        moment = moment + dot(xv[:, cols], gv[...], 0, 0)
        for o in range(NF - 1):
            moment = moment + dot(xr[o, :, 256 * s : 256 * s + 256], gr[o], 0, 0)
        cs = (csh[pl.ds(own + 64 * s, 64), :], csl[pl.ds(own + 64 * s, 64), :])
        coeff = lanes_transform(dot3(cs, split(moment)), table, 1)
        coeff = jnp.where(lane512 == jrow[pl.ds(own + 64 * s, 64), :1], coeff, 0.0)
        chosen = dot3(cs, split(lanes_transform(coeff, table, 0)), 0, 0)
        mout[256 * s : 256 * s + 256, :] = (moment - chosen).astype(BF)
        copy = pltpu.make_async_copy(
            mout.at[pl.ds(256 * s, 256), :], out_m.at[pl.ds(256 * s, 256), :], lsem.at[1 + s]
        )
        copy.start()
        m_out.append(copy)
    for copy in m_out:
        copy.wait()
    u_out.wait()
    for copy in sends:
        copy.wait_send()


def body(activations, output_grads, momentum, chosen_blocks):
    high, low = tables()
    picks = jnp.pad(chosen_blocks[0].astype(BF), ((0, 0), (0, 120)))
    dma = pltpu.SemaphoreType.DMA
    vmem = pl.BlockSpec(memory_space=pltpu.VMEM)
    anywhere = pl.BlockSpec(memory_space=pl.ANY)
    scratch = [
        pltpu.VMEM((256, 4096), BF),
        pltpu.VMEM((256, 512), BF),
        pltpu.VMEM((1024, 512), BF),
        pltpu.VMEM((3, 256, 1024), BF),
        pltpu.VMEM((3, 256, 512), BF),
        pltpu.VMEM((4, 16, 128), BF),
        pltpu.VMEM((1024, 256), BF),
        pltpu.VMEM((1024, 256), BF),
        pltpu.VMEM((1024, 128), F32),
        pltpu.VMEM((1024, 128), F32),
        pltpu.VMEM((4, 128, 128), F32),
        pltpu.VMEM((4, 128, 128), BF),
        pltpu.VMEM((3, 128, 128), BF),
        pltpu.VMEM((256, 128), BF),
        pltpu.VMEM((8, 32, 128), BF),
        pltpu.VMEM((8, 64, 128), BF),
        pltpu.VMEM((7, 64, 128), BF),
        pltpu.VMEM((3, 64, 128), BF),
        pltpu.VMEM((1024, 512), BF),
        pltpu.VMEM((1024, 512), BF),
        dma((5,)),
        dma((3,)), dma((3,)), dma((12,)), dma((12,)), dma((3,)), dma((3,)),
        dma((3,)), dma((3,)), dma((7,)), dma((7,)), dma((7,)), dma((7,)),
        dma((2,)), dma((2,)), dma((7,)), dma((7,)), dma((3,)), dma((3,)),
        dma((4,)), dma((4,)),
    ]
    moment_next, update = pl.pallas_call(
        kernel,
        out_shape=(
            jax.ShapeDtypeStruct((1024, 512), BF),
            jax.ShapeDtypeStruct((1024, 512), BF),
        ),
        in_specs=[anywhere, anywhere, anywhere, vmem, vmem, vmem, vmem, vmem],
        out_specs=(anywhere, anywhere),
        scratch_shapes=scratch,
        compiler_params=pltpu.CompilerParams(
            collective_id=0, has_side_effects=True, vmem_limit_bytes=48 * 1024 * 1024
        ),
        name="step",
    )(
        activations, output_grads, momentum[0], picks,
        jnp.asarray(high), jnp.asarray(low), jnp.asarray(high.T), jnp.asarray(low.T),
    )
    return (moment_next[None], update.astype(F32))


def solution(mesh):
    return jax.shard_map(
        body,
        mesh=mesh,
        in_specs=(
            P(("replica", "fsdp"), None),
            P(("replica", "fsdp"), None),
            P("replica", "fsdp", None),
            P("replica", "fsdp", None),
        ),
        out_specs=(P("replica", "fsdp", None), P("fsdp", None)),
        check_vma=False,
    )
```

```python
import math

import jax
import jax.numpy as jnp
import numpy as np
from jax import lax
from jax.experimental import pallas as pl
from jax.experimental.pallas import tpu as pltpu
from jax.sharding import PartitionSpec as P

MESH = pl.DeviceIdType.MESH
F32 = jnp.float32
BF = jnp.bfloat16
SPAN = 64
NX, NY, NZ, NF = 8, 8, 3, 4
SLABS = 4
PIECES = 8


def tables():
    order = np.arange(SPAN)[:, None]
    place = np.arange(SPAN)[None, :]
    factor = np.where(order == 0, math.sqrt(1.0 / SPAN), math.sqrt(2.0 / SPAN))
    table = factor * np.cos(np.pi * (2 * place + 1) * order / (2 * SPAN))
    block = np.kron(np.eye(4), table).astype(np.float32)
    high = block.astype(jnp.bfloat16)
    low = (block - high.astype(np.float32)).astype(jnp.bfloat16)
    return high, low


def dot(a, b, ca=1, cb=0):
    return lax.dot_general(a, b, (((ca,), (cb,)), ((), ())), preferred_element_type=F32)


def split(a):
    high = a.astype(BF)
    return high, (a - high.astype(F32)).astype(BF)


def dot3(a, b, ca=1, cb=0):
    return dot(a[0], b[0], ca, cb) + dot(a[0], b[1], ca, cb) + dot(a[1], b[0], ca, cb)


def lanes_transform(value, table, cb):
    high, low = split(value)
    width = value.shape[1] // 256
    return jnp.concatenate(
        [
            dot3((high[:, 256 * t : 256 * t + 256], low[:, 256 * t : 256 * t + 256]), table, 1, cb)
            for t in range(width)
        ],
        axis=1,
    )


def iota(shape, dim):
    return lax.broadcasted_iota(jnp.int32, shape, dim)


def fold(value, span_col):
    lane = iota((value.shape[0], 128), 1)
    half = jnp.floor(span_col * 0.5)
    odd = span_col - 2.0 * half
    kept = jnp.zeros((value.shape[0], 128), F32)
    for s in range(4):
        kept = kept + jnp.where(half == float(s), value[:, 128 * s : 128 * s + 128], 0.0)
    kept = jnp.where((lane >> 6).astype(F32) == odd, kept, 0.0)
    return kept + pltpu.roll(kept, 64, 1)


def pack(rows):
    lane = iota((128, 128), 1)
    return jnp.where(lane < 64, rows[:128], rows[128:])


def kernel(
    x_hbm, g_hbm, mom_hbm, pk_hbm, tab_hbm,
    out_m, out_u,
    xv, g_all, mv, tab, xr, pk_all, csh, csl, jrow, trow, upart, usend, urecv,
    sent, a2, dp, by, zb, fin,
    lsem, pk_s, pk_r, x_s, x_r, g_s, g_r, u_s, u_r, a_s, a_r, b_s, b_r,
    z_s, z_r, y_s, y_r, w_s, w_r, c_s, c_r,
):
    rep = lax.axis_index("replica")
    f = lax.axis_index("fsdp")
    m = lax.rem(rep, NX)
    row = rep - m
    y = lax.rem(lax.div(rep, NX), NY)
    zh = lax.div(rep, NX * NY)
    plane = lax.rem(rep, NX * NY)

    def line_peer(o):
        return (rep, lax.rem(f + o, NF))

    def row_peer(o):
        return (row + lax.rem(m + o, NX), f)

    def col_peer(o):
        return (zh * (NX * NY) + lax.rem(y + o, NY) * NX + m, f)

    def hi_peer(o):
        return (lax.rem(zh + o, NZ) * (NX * NY) + plane, f)

    loads = [
        pltpu.make_async_copy(x_hbm, xv, lsem.at[0]),
        pltpu.make_async_copy(g_hbm, g_all.at[f], lsem.at[1]),
        pltpu.make_async_copy(mom_hbm.at[0], mv, lsem.at[2]),
        pltpu.make_async_copy(tab_hbm, tab, lsem.at[3]),
        pltpu.make_async_copy(pk_hbm, pk_all.at[f], lsem.at[4]),
    ]
    for copy in loads:
        copy.start()

    barrier = pltpu.get_barrier_semaphore()
    for make, count in ((line_peer, NF), (row_peer, NX), (col_peer, NY), (hi_peer, NZ)):
        for o in range(1, count):
            pl.semaphore_signal(barrier, inc=1, device_id=make(o), device_id_type=MESH)
    pl.semaphore_wait(barrier, NF + NX + NY + NZ - 4)

    sends = []

    def remote(src, dst, ssem, rsem, peer):
        copy = pltpu.make_async_remote_copy(
            src_ref=src, dst_ref=dst, send_sem=ssem, recv_sem=rsem,
            device_id=peer, device_id_type=MESH,
        )
        copy.start()
        sends.append(copy)
        return copy

    pk_copies = [
        remote(pk_hbm, pk_all.at[f], pk_s.at[o - 1], pk_r.at[o - 1], line_peer(o))
        for o in range(1, NF)
    ]

    x_copies = []

    def send_x(count):
        for piece in range(len(x_copies), len(x_copies) + count):
            out = []
            for o in range(1, NF):
                peer = lax.rem(f + o, NF)
                cols = pl.ds(pl.multiple_of(peer * 1024 + piece * 128, 128), 128)
                k = piece * 3 + o - 1
                out.append(
                    remote(
                        x_hbm.at[:, cols], xr.at[o - 1, :, pl.ds(piece * 128, 128)],
                        x_s.at[k], x_r.at[k], line_peer(o),
                    )
                )
            x_copies.append(out)

    def relay(hop, direction):
        step = 1 - 2 * direction
        source = f - step * hop
        present = (source >= 0) & (source < NF)
        onward = present & (f + step >= 0) & (f + step < NF)
        slot = lax.rem(source + NF, NF)
        copy = pltpu.make_async_remote_copy(
            src_ref=g_all.at[slot], dst_ref=g_all.at[slot],
            send_sem=g_s.at[direction * 3 + lax.rem(hop, 3)], recv_sem=g_r.at[direction * 3 + hop],
            device_id=(rep, lax.rem(f + step + NF, NF)), device_id_type=MESH,
        )
        return present, onward, copy

    def send_g(hop):
        for direction in range(2):
            _, onward, copy = relay(hop, direction)

            @pl.when(onward)
            def _():
                copy.start()

    def wait_g(hop):
        for direction in range(2):
            step = 1 - 2 * direction
            source = f - step * hop
            slot = lax.rem(source + NF, NF)

            @pl.when((source >= 0) & (source < NF))
            def _():
                pltpu.make_async_remote_copy(
                    src_ref=g_all.at[slot], dst_ref=g_all.at[slot],
                    send_sem=g_s.at[direction * 3], recv_sem=g_r.at[direction * 3 + hop - 1],
                    device_id=(rep, lax.rem(f + step + NF, NF)), device_id_type=MESH,
                ).wait_recv()


    for copy in (loads[1], loads[3], loads[4]):
        copy.wait()
    send_g(0)
    send_x(1)
    table = (tab[0], tab[1])
    gv = g_all[f]
    gc = split(
        jnp.concatenate(
            [
                dot(gv[:, 256 * t : 256 * t + 256], table[0], 1, 1)
                + dot(gv[:, 256 * t : 256 * t + 256], table[1], 1, 1)
                for t in range(2)
            ],
            axis=1,
        )
    )
    for copy in pk_copies:
        copy.wait_recv()

    rows = iota((256, 128), 0)
    lane = iota((256, 128), 1)
    pick_lane = lane == ((rows >> 1) & 7)
    spread = (iota((256, 16), 1) == (iota((256, 16), 0) >> 4)).astype(BF)
    odd_row = (rows & 1).astype(F32)
    lane2 = iota((256, 256), 1).astype(F32)
    shift = (((iota((256, 1), 0) >> 4) & 3) * 64).astype(F32)
    loads[0].wait()
    for fi in range(NF):
        at = pl.ds(fi * 256, 256)
        number = jnp.sum(jnp.where(pick_lane, dot(spread, pk_all[fi]), 0.0), axis=1, keepdims=True)
        col = jnp.floor(number * (1.0 / 32.0))
        coeff_row = 2.0 * (number - 32.0 * col) + odd_row[:, :1]
        onehot = jnp.where(lane2 == coeff_row + shift, 1.0, 0.0).astype(BF)
        cs_high = dot(onehot, table[0]).astype(BF)
        cs_low = dot(onehot, table[1]).astype(BF)
        csh[at, :] = cs_high
        csl[at, :] = cs_low
        col_b = jnp.broadcast_to(col, (256, 128))
        jrow[at, :] = col_b
        trow[at, :] = jnp.broadcast_to(coeff_row + 64.0 * jnp.floor(col * 0.5), (256, 128))
        parts = []
        for s in range(SLABS):
            xs = xv[:, (fi * SLABS + s) * 256 : (fi * SLABS + s + 1) * 256]
            parts.append(
                dot(cs_high[64 * s : 64 * s + 64], xs, 1, 1)
                + dot(cs_low[64 * s : 64 * s + 64], xs, 1, 1)
            )
        value = dot3(split(jnp.concatenate(parts, axis=0)), gc)
        packed = pack(fold(value, col_b))
        upart[fi] = packed
        usend[fi] = packed.astype(BF)

    u_copies = [
        remote(
            usend.at[lax.rem(f + o, NF)], urecv.at[o - 1], u_s.at[o - 1], u_r.at[o - 1], line_peer(o)
        )
        for o in range(1, NF)
    ]
    wait_g(1)
    send_g(1)
    send_x(2)

    own = pl.multiple_of(f * 256, 256)
    loads[2].wait()
    parts = []
    for s in range(SLABS):
        high = csh[pl.ds(own + 64 * s, 64), :]
        low = csl[pl.ds(own + 64 * s, 64), :]
        ms = mv[256 * s : 256 * s + 256, :]
        parts.append(dot(high, ms) + dot(low, ms))
    col_b = jrow[pl.ds(own, 256), :]
    from_momentum = fold(lanes_transform(jnp.concatenate(parts, axis=0), table, 1), col_b)
    packed = upart[f] + 0.9 * pack(from_momentum)
    for copy in u_copies:
        copy.wait_recv()
    for o in range(3):
        packed = packed + urecv[o].astype(F32)
    packed = jnp.concatenate([packed, pltpu.roll(packed, 64, 1)], axis=0)
    col_odd = col_b - 2.0 * jnp.floor(col_b * 0.5)
    tile = jnp.where(lane < 64, packed, jnp.where(lane < 96, trow[pl.ds(own, 256), :], col_odd))
    sent[...] = tile.astype(BF)

    a_copies = []
    for o in range(1, NX):
        there = pl.ds(pl.multiple_of(lax.rem(m + o, NX) * 32, 32), 32)
        a_copies.append(
            remote(sent.at[there, :], a2.at[o - 1], a_s.at[o - 1], a_r.at[o - 1], row_peer(o))
        )
    a2[NX - 1] = sent[pl.ds(pl.multiple_of(m * 32, 32), 32), :]
    for copy in a_copies:
        copy.wait_recv()
    lane1 = iota((128, 128), 1)
    lane256 = iota((128, 256), 1).astype(F32)
    for u in range(2):
        got = jnp.concatenate(
            [a2[o, 16 * u : 16 * u + 16, :] for o in range(NX)], axis=0
        ).astype(F32)
        value = jnp.where(lane1 < 64, got, 0.0)
        value = value + pltpu.roll(value, 64, 1)
        value = jnp.where((lane1 >> 6).astype(F32) == got[:, 96:97], value, 0.0)
        onehot = jnp.where(lane256 == got[:, 64:65], 1.0, 0.0)
        dense = dot(onehot.astype(BF), value.astype(BF), 0, 0).astype(BF)
        for s in range(4):
            dp[4 * u + s] = dense[64 * s : 64 * s + 64]
    b_copies = [
        remote(
            dp.at[lax.rem(y + o, NY)], by.at[o - 1], b_s.at[o - 1], b_r.at[o - 1], col_peer(o)
        )
        for o in range(1, NY)
    ]
    plane_sum = dp[y].astype(F32)
    for copy in b_copies:
        copy.wait_recv()
    for o in range(NY - 1):
        plane_sum = plane_sum + by[o].astype(F32)
    zb[zh] = plane_sum.astype(BF)
    z_copies = [
        remote(zb.at[zh], zb.at[zh], z_s.at[o - 1], z_r.at[o - 1], hi_peer(o))
        for o in range(1, NZ)
    ]
    wait_g(2)
    send_g(2)
    send_x(5)
    for copy in z_copies:
        copy.wait_recv()
    total = zb[0].astype(F32) + zb[1].astype(F32) + zb[2].astype(F32)
    left = dot3((tab[2, :64, :64], tab[3, :64, :64]), split(total))
    piece = dot3(split(left), (tab[0, :128, :128], tab[1, :128, :128]))
    piece_rows = pl.ds(pl.multiple_of(m * 128 + lax.div(y, 4) * 64, 64), 64)
    piece_cols = pl.ds(pl.multiple_of(lax.rem(y, 4) * 128, 128), 128)
    fin[piece_rows, piece_cols] = piece.astype(BF)
    y_copies = [
        remote(
            fin.at[piece_rows, piece_cols], fin.at[piece_rows, piece_cols],
            y_s.at[o - 1], y_r.at[o - 1], col_peer(o),
        )
        for o in range(1, NY)
    ]
    lane512 = (iota((64, 512), 1) >> 6).astype(F32)

    def slab(s):
        for piece in (2 * s, 2 * s + 1):
            for copy in x_copies[piece]:
                copy.wait_recv()
        cols = pl.ds(pl.multiple_of(f * 1024 + s * 256, 256), 256)
        moment = 0.9 * mv[256 * s : 256 * s + 256, :].astype(F32)
        moment = moment + dot(xv[:, cols], g_all[f], 0, 0)
        for o in range(1, NF):
            source = lax.rem(f + NF - o, NF)
            moment = moment + dot(xr[o - 1, :, 256 * s : 256 * s + 256], g_all[source], 0, 0)
        cs = (csh[pl.ds(own + 64 * s, 64), :], csl[pl.ds(own + 64 * s, 64), :])
        coeff = lanes_transform(dot3(cs, split(moment)), table, 1)
        coeff = jnp.where(lane512 == jrow[pl.ds(own + 64 * s, 64), :1], coeff, 0.0)
        chosen = dot3(cs, split(lanes_transform(coeff, table, 0)), 0, 0)
        out_m[256 * s : 256 * s + 256, :] = (moment - chosen).astype(BF)

    for copy in y_copies:
        copy.wait_recv()
    band = pl.ds(pl.multiple_of(m * 128, 128), 128)
    w_copies = [
        remote(fin.at[band, :], fin.at[band, :], w_s.at[o - 1], w_r.at[o - 1], row_peer(2 * o))
        for o in range(1, 4)
    ]
    other = (row + m + 1 - 2 * lax.rem(m, 2), f)
    c_copies = [remote(fin.at[band, :], fin.at[band, :], c_s.at[0], c_r.at[0], other)]
    wait_g(3)
    slab(0)
    for o in range(1, 4):
        w_copies[o - 1].wait_recv()
        there = pl.ds(pl.multiple_of(lax.rem(m + NX - 2 * o, NX) * 128, 128), 128)
        c_copies.append(remote(fin.at[there, :], fin.at[there, :], c_s.at[o], c_r.at[o], other))
    slab(1)
    for copy in c_copies:
        copy.wait_recv()
    out_u[...] = fin[...]

    slab(2)
    slab(3)
    for copy in sends:
        copy.wait_send()
    for hop in range(3):
        for direction in range(2):
            _, onward, copy = relay(hop, direction)

            @pl.when(onward)
            def _():
                copy.wait_send()


def body(activations, output_grads, momentum, chosen_blocks):
    high, low = tables()
    picks = jnp.pad(chosen_blocks[0].astype(BF), ((0, 0), (0, 120)))
    dma = pltpu.SemaphoreType.DMA
    anywhere = pl.BlockSpec(memory_space=pl.ANY)
    scratch = [
        pltpu.VMEM((256, 4096), BF),
        pltpu.VMEM((4, 256, 512), BF),
        pltpu.VMEM((1024, 512), BF),
        pltpu.VMEM((4, 256, 256), BF),
        pltpu.VMEM((3, 256, 1024), BF),
        pltpu.VMEM((4, 16, 128), BF),
        pltpu.VMEM((1024, 256), BF),
        pltpu.VMEM((1024, 256), BF),
        pltpu.VMEM((1024, 128), F32),
        pltpu.VMEM((1024, 128), F32),
        pltpu.VMEM((4, 128, 128), F32),
        pltpu.VMEM((4, 128, 128), BF),
        pltpu.VMEM((3, 128, 128), BF),
        pltpu.VMEM((256, 128), BF),
        pltpu.VMEM((8, 32, 128), BF),
        pltpu.VMEM((8, 64, 128), BF),
        pltpu.VMEM((7, 64, 128), BF),
        pltpu.VMEM((3, 64, 128), BF),
        pltpu.VMEM((1024, 512), BF),
        dma((5,)),
        dma((3,)), dma((3,)), dma((24,)), dma((24,)), dma((6,)), dma((6,)),
        dma((3,)), dma((3,)), dma((7,)), dma((7,)), dma((7,)), dma((7,)),
        dma((2,)), dma((2,)), dma((7,)), dma((7,)), dma((3,)), dma((3,)),
        dma((4,)), dma((4,)),
    ]
    moment_next, update = pl.pallas_call(
        kernel,
        out_shape=(
            jax.ShapeDtypeStruct((1024, 512), BF),
            jax.ShapeDtypeStruct((1024, 512), BF),
        ),
        in_specs=[anywhere] * 5,
        out_specs=(pl.BlockSpec(memory_space=pltpu.VMEM),) * 2,
        scratch_shapes=scratch,
        compiler_params=pltpu.CompilerParams(
            collective_id=0, has_side_effects=True, vmem_limit_bytes=62 * 1024 * 1024
        ),
        name="step",
    )(
        activations, output_grads, momentum, picks,
        jnp.asarray(np.stack([high, low, high.T, low.T])),
    )
    return (moment_next[None], update.astype(F32))


def solution(mesh):
    return jax.shard_map(
        body,
        mesh=mesh,
        in_specs=(
            P(("replica", "fsdp"), None),
            P(("replica", "fsdp"), None),
            P("replica", "fsdp", None),
            P("replica", "fsdp", None),
        ),
        out_specs=(P("replica", "fsdp", None), P("fsdp", None)),
        check_vma=False,
    )
```

```python
import math

import jax
import jax.numpy as jnp
import numpy as np
from jax import lax
from jax.experimental import pallas as pl
from jax.experimental.pallas import tpu as pltpu
from jax.sharding import PartitionSpec as P

MESH = pl.DeviceIdType.MESH
F32 = jnp.float32
BF = jnp.bfloat16
SPAN = 64
NX, NY, NZ, NF = 8, 8, 3, 4
SLABS = 4
PIECES = 8


def tables():
    order = np.arange(SPAN)[:, None]
    place = np.arange(SPAN)[None, :]
    factor = np.where(order == 0, math.sqrt(1.0 / SPAN), math.sqrt(2.0 / SPAN))
    table = factor * np.cos(np.pi * (2 * place + 1) * order / (2 * SPAN))
    block = np.kron(np.eye(4), table).astype(np.float32)
    high = block.astype(jnp.bfloat16)
    low = (block - high.astype(np.float32)).astype(jnp.bfloat16)
    return high, low


def dot(a, b, ca=1, cb=0):
    return lax.dot_general(a, b, (((ca,), (cb,)), ((), ())), preferred_element_type=F32)


def split(a):
    high = a.astype(BF)
    return high, (a - high.astype(F32)).astype(BF)


def dot3(a, b, ca=1, cb=0):
    return dot(a[0], b[0], ca, cb) + dot(a[0], b[1], ca, cb) + dot(a[1], b[0], ca, cb)


def lanes_transform(value, table, cb):
    high, low = split(value)
    width = value.shape[1] // 256
    return jnp.concatenate(
        [
            dot3((high[:, 256 * t : 256 * t + 256], low[:, 256 * t : 256 * t + 256]), table, 1, cb)
            for t in range(width)
        ],
        axis=1,
    )


def iota(shape, dim):
    return lax.broadcasted_iota(jnp.int32, shape, dim)


def fold(value, span_col):
    lane = iota((value.shape[0], 128), 1)
    half = jnp.floor(span_col * 0.5)
    odd = span_col - 2.0 * half
    kept = jnp.zeros((value.shape[0], 128), F32)
    for s in range(4):
        kept = kept + jnp.where(half == float(s), value[:, 128 * s : 128 * s + 128], 0.0)
    kept = jnp.where((lane >> 6).astype(F32) == odd, kept, 0.0)
    return kept + pltpu.roll(kept, 64, 1)


def pack(rows):
    lane = iota((128, 128), 1)
    return jnp.where(lane < 64, rows[:128], rows[128:])


def kernel(
    x_hbm, g_hbm, mom_hbm, pk_hbm, tab_hbm,
    out_m, out_u,
    xv, g_all, mv, tab, xr, pk_own, pk_all, csh, csl, jrow, trow, upart, usend, urecv,
    sent, a2, dp, by, zb, fin,
    gate, lsem, pk_s, pk_r, x_s, x_r, g_s, g_r, u_s, u_r, a_s, a_r, b_s, b_r,
    z_s, z_r, y_s, y_r, w_s, w_r, c_s, c_r,
):
    rep = lax.axis_index("replica")
    f = lax.axis_index("fsdp")
    m = lax.rem(rep, NX)
    row = rep - m
    y = lax.rem(lax.div(rep, NX), NY)
    zh = lax.div(rep, NX * NY)
    plane = lax.rem(rep, NX * NY)

    def line_peer(o):
        return (rep, lax.rem(f + o, NF))

    def row_peer(o):
        return (row + lax.rem(m + o, NX), f)

    def col_peer(o):
        return (zh * (NX * NY) + lax.rem(y + o, NY) * NX + m, f)

    def hi_peer(o):
        return (lax.rem(zh + o, NZ) * (NX * NY) + plane, f)

    loads = [
        pltpu.make_async_copy(x_hbm, xv, lsem.at[0]),
        pltpu.make_async_copy(g_hbm, g_all.at[f], lsem.at[1]),
        pltpu.make_async_copy(mom_hbm.at[0], mv, lsem.at[2]),
        pltpu.make_async_copy(tab_hbm, tab, lsem.at[3]),
        pltpu.make_async_copy(pk_hbm, pk_own, lsem.at[4]),
    ]
    for copy in loads:
        copy.start()

    barrier = pltpu.get_barrier_semaphore()
    core = lax.rem(m, 2)
    other = (rep + 1 - 2 * core, f)

    def enter(there):
        pl.semaphore_signal(barrier, inc=1, device_id=there, device_id_type=MESH)

    for o in range(1, NF):
        enter((rep - core, lax.rem(f + o, NF)))
    for o in range(2, NX, 2):
        enter((row + lax.rem(m - core + o, NX), f))
    for o in range(1, NY):
        enter((zh * (NX * NY) + lax.rem(y + o, NY) * NX + m - core, f))
    for o in range(1, NZ):
        enter((lax.rem(zh + o, NZ) * (NX * NY) + plane - core + 1, f))

    @pl.when(core == 1)
    def _():
        enter(other)

    for copy in (loads[4],):
        copy.wait()
    pk_all[f] = jnp.zeros((8, 128), F32)
    pk_all[f, :, :16] = pk_own[...].astype(F32)

    @pl.when(core == 0)
    def _():
        pl.semaphore_wait(barrier, 2 * (NF - 1) + (NX - 1) + 2 * (NY - 1))
        pl.semaphore_signal(gate, inc=1, device_id=other, device_id_type=MESH)

    @pl.when(core == 1)
    def _():
        pl.semaphore_wait(gate, 1)

    sends = []

    def remote(src, dst, ssem, rsem, peer):
        copy = pltpu.make_async_remote_copy(
            src_ref=src, dst_ref=dst, send_sem=ssem, recv_sem=rsem,
            device_id=peer, device_id_type=MESH,
        )
        copy.start()
        sends.append(copy)
        return copy

    pk_copies = [
        remote(pk_all.at[f], pk_all.at[f], pk_s.at[o - 1], pk_r.at[o - 1], line_peer(o))
        for o in range(1, NF)
    ]

    x_copies = []

    def send_x(count):
        for piece in range(len(x_copies), len(x_copies) + count):
            out = []
            for o in range(1, NF):
                peer = lax.rem(f + o, NF)
                cols = pl.ds(pl.multiple_of(peer * 1024 + piece * 128, 128), 128)
                k = piece * 3 + o - 1
                out.append(
                    remote(
                        x_hbm.at[:, cols], xr.at[o - 1, :, pl.ds(piece * 128, 128)],
                        x_s.at[k], x_r.at[k], line_peer(o),
                    )
                )
            x_copies.append(out)

    def relay(hop, direction):
        step = 1 - 2 * direction
        source = f - step * hop
        present = (source >= 0) & (source < NF)
        onward = present & (f + step >= 0) & (f + step < NF)
        slot = lax.rem(source + NF, NF)
        copy = pltpu.make_async_remote_copy(
            src_ref=g_all.at[slot], dst_ref=g_all.at[slot],
            send_sem=g_s.at[direction * 3 + lax.rem(hop, 3)], recv_sem=g_r.at[direction * 3 + hop],
            device_id=(rep, lax.rem(f + step + NF, NF)), device_id_type=MESH,
        )
        return present, onward, copy

    def send_g(hop):
        for direction in range(2):
            _, onward, copy = relay(hop, direction)

            @pl.when(onward)
            def _():
                copy.start()

    def wait_g(hop):
        for direction in range(2):
            step = 1 - 2 * direction
            source = f - step * hop
            slot = lax.rem(source + NF, NF)

            @pl.when((source >= 0) & (source < NF))
            def _():
                pltpu.make_async_remote_copy(
                    src_ref=g_all.at[slot], dst_ref=g_all.at[slot],
                    send_sem=g_s.at[direction * 3], recv_sem=g_r.at[direction * 3 + hop - 1],
                    device_id=(rep, lax.rem(f + step + NF, NF)), device_id_type=MESH,
                ).wait_recv()


    for copy in (loads[1], loads[3]):
        copy.wait()
    send_g(0)
    send_x(1)
    table = (tab[0], tab[1])
    gv = g_all[f]
    gc = split(
        jnp.concatenate(
            [
                dot(gv[:, 256 * t : 256 * t + 256], table[0], 1, 1)
                + dot(gv[:, 256 * t : 256 * t + 256], table[1], 1, 1)
                for t in range(2)
            ],
            axis=1,
        )
    )
    for copy in pk_copies:
        copy.wait_recv()

    rows = iota((256, 128), 0)
    lane = iota((256, 128), 1)
    pick_lane = lane == (rows >> 4)
    spread = (iota((256, 8), 1) == ((iota((256, 8), 0) >> 1) & 7)).astype(BF)
    odd_row = (rows & 1).astype(F32)
    lane2 = iota((256, 256), 1).astype(F32)
    shift = (((iota((256, 1), 0) >> 4) & 3) * 64).astype(F32)
    loads[0].wait()
    for fi in range(NF):
        at = pl.ds(fi * 256, 256)
        number = jnp.sum(jnp.where(pick_lane, dot(spread, pk_all[fi].astype(BF)), 0.0), axis=1, keepdims=True)
        col = jnp.floor(number * (1.0 / 32.0))
        coeff_row = 2.0 * (number - 32.0 * col) + odd_row[:, :1]
        onehot = jnp.where(lane2 == coeff_row + shift, 1.0, 0.0).astype(BF)
        cs_high = dot(onehot, table[0]).astype(BF)
        cs_low = dot(onehot, table[1]).astype(BF)
        csh[at, :] = cs_high
        csl[at, :] = cs_low
        col_b = jnp.broadcast_to(col, (256, 128))
        jrow[at, :] = col_b
        trow[at, :] = jnp.broadcast_to(coeff_row + 64.0 * jnp.floor(col * 0.5), (256, 128))
        parts = []
        for s in range(SLABS):
            xs = xv[:, (fi * SLABS + s) * 256 : (fi * SLABS + s + 1) * 256]
            parts.append(
                dot(cs_high[64 * s : 64 * s + 64], xs, 1, 1)
                + dot(cs_low[64 * s : 64 * s + 64], xs, 1, 1)
            )
        value = dot3(split(jnp.concatenate(parts, axis=0)), gc)
        packed = pack(fold(value, col_b))
        upart[fi] = packed
        usend[fi] = packed.astype(BF)

    u_copies = [
        remote(
            usend.at[lax.rem(f + o, NF)], urecv.at[o - 1], u_s.at[o - 1], u_r.at[o - 1], line_peer(o)
        )
        for o in range(1, NF)
    ]
    wait_g(1)
    send_g(1)
    send_x(2)

    own = pl.multiple_of(f * 256, 256)
    loads[2].wait()
    parts = []
    for s in range(SLABS):
        high = csh[pl.ds(own + 64 * s, 64), :]
        low = csl[pl.ds(own + 64 * s, 64), :]
        ms = mv[256 * s : 256 * s + 256, :]
        parts.append(dot(high, ms) + dot(low, ms))
    col_b = jrow[pl.ds(own, 256), :]
    from_momentum = fold(lanes_transform(jnp.concatenate(parts, axis=0), table, 1), col_b)
    packed = upart[f] + 0.9 * pack(from_momentum)
    for copy in u_copies:
        copy.wait_recv()
    for o in range(3):
        packed = packed + urecv[o].astype(F32)
    packed = jnp.concatenate([packed, pltpu.roll(packed, 64, 1)], axis=0)
    col_odd = col_b - 2.0 * jnp.floor(col_b * 0.5)
    tile = jnp.where(lane < 64, packed, jnp.where(lane < 96, trow[pl.ds(own, 256), :], col_odd))
    sent[...] = tile.astype(BF)

    a_copies = []
    for o in range(1, NX):
        there = pl.ds(pl.multiple_of(lax.rem(m + o, NX) * 32, 32), 32)
        a_copies.append(
            remote(sent.at[there, :], a2.at[o - 1], a_s.at[o - 1], a_r.at[o - 1], row_peer(o))
        )
    a2[NX - 1] = sent[pl.ds(pl.multiple_of(m * 32, 32), 32), :]
    for copy in a_copies:
        copy.wait_recv()
    lane1 = iota((128, 128), 1)
    lane256 = iota((128, 256), 1).astype(F32)
    for u in range(2):
        got = jnp.concatenate(
            [a2[o, 16 * u : 16 * u + 16, :] for o in range(NX)], axis=0
        ).astype(F32)
        value = jnp.where(lane1 < 64, got, 0.0)
        value = value + pltpu.roll(value, 64, 1)
        value = jnp.where((lane1 >> 6).astype(F32) == got[:, 96:97], value, 0.0)
        onehot = jnp.where(lane256 == got[:, 64:65], 1.0, 0.0)
        dense = dot(onehot.astype(BF), value.astype(BF), 0, 0).astype(BF)
        for s in range(4):
            dp[4 * u + s] = dense[64 * s : 64 * s + 64]
    b_copies = [
        remote(
            dp.at[lax.rem(y + o, NY)], by.at[o - 1], b_s.at[o - 1], b_r.at[o - 1], col_peer(o)
        )
        for o in range(1, NY)
    ]
    plane_sum = dp[y].astype(F32)
    for copy in b_copies:
        copy.wait_recv()
    for o in range(NY - 1):
        plane_sum = plane_sum + by[o].astype(F32)
    zb[zh] = plane_sum.astype(BF)

    @pl.when(core == 1)
    def _():
        pl.semaphore_wait(barrier, 2 * (NZ - 1))
        pl.semaphore_signal(gate, inc=1, device_id=other, device_id_type=MESH)

    @pl.when(core == 0)
    def _():
        pl.semaphore_wait(gate, 1)

    z_copies = [
        remote(zb.at[zh], zb.at[zh], z_s.at[o - 1], z_r.at[o - 1], hi_peer(o))
        for o in range(1, NZ)
    ]
    wait_g(2)
    send_g(2)
    send_x(5)
    for copy in z_copies:
        copy.wait_recv()
    total = zb[0].astype(F32) + zb[1].astype(F32) + zb[2].astype(F32)
    left = dot3((tab[2, :64, :64], tab[3, :64, :64]), split(total))
    piece = dot3(split(left), (tab[0, :128, :128], tab[1, :128, :128]))
    piece_rows = pl.ds(pl.multiple_of(m * 128 + lax.div(y, 4) * 64, 64), 64)
    piece_cols = pl.ds(pl.multiple_of(lax.rem(y, 4) * 128, 128), 128)
    fin[piece_rows, piece_cols] = piece.astype(BF)
    y_copies = [
        remote(
            fin.at[piece_rows, piece_cols], fin.at[piece_rows, piece_cols],
            y_s.at[o - 1], y_r.at[o - 1], col_peer(o),
        )
        for o in range(1, NY)
    ]
    lane512 = (iota((64, 512), 1) >> 6).astype(F32)

    def slab(s):
        for piece in (2 * s, 2 * s + 1):
            for copy in x_copies[piece]:
                copy.wait_recv()
        cols = pl.ds(pl.multiple_of(f * 1024 + s * 256, 256), 256)
        moment = 0.9 * mv[256 * s : 256 * s + 256, :].astype(F32)
        moment = moment + dot(xv[:, cols], g_all[f], 0, 0)
        for o in range(1, NF):
            source = lax.rem(f + NF - o, NF)
            moment = moment + dot(xr[o - 1, :, 256 * s : 256 * s + 256], g_all[source], 0, 0)
        cs = (csh[pl.ds(own + 64 * s, 64), :], csl[pl.ds(own + 64 * s, 64), :])
        coeff = lanes_transform(dot3(cs, split(moment)), table, 1)
        coeff = jnp.where(lane512 == jrow[pl.ds(own + 64 * s, 64), :1], coeff, 0.0)
        chosen = dot3(cs, split(lanes_transform(coeff, table, 0)), 0, 0)
        out_m[256 * s : 256 * s + 256, :] = (moment - chosen).astype(BF)

    for copy in y_copies:
        copy.wait_recv()
    band = pl.ds(pl.multiple_of(m * 128, 128), 128)
    w_copies = [
        remote(fin.at[band, :], fin.at[band, :], w_s.at[o - 1], w_r.at[o - 1], row_peer(2 * o))
        for o in range(1, 4)
    ]
    c_copies = [remote(fin.at[band, :], fin.at[band, :], c_s.at[0], c_r.at[0], other)]
    wait_g(3)
    slab(0)
    for o in range(1, 4):
        w_copies[o - 1].wait_recv()
        there = pl.ds(pl.multiple_of(lax.rem(m + NX - 2 * o, NX) * 128, 128), 128)
        c_copies.append(remote(fin.at[there, :], fin.at[there, :], c_s.at[o], c_r.at[o], other))
    slab(1)
    for copy in c_copies:
        copy.wait_recv()
    out_u[...] = fin[...]

    slab(2)
    slab(3)
    for copy in sends:
        copy.wait_send()
    for hop in range(3):
        for direction in range(2):
            _, onward, copy = relay(hop, direction)

            @pl.when(onward)
            def _():
                copy.wait_send()


def body(activations, output_grads, momentum, chosen_blocks):
    high, low = tables()
    picks = chosen_blocks[0].T
    dma = pltpu.SemaphoreType.DMA
    anywhere = pl.BlockSpec(memory_space=pl.ANY)
    scratch = [
        pltpu.VMEM((256, 4096), BF),
        pltpu.VMEM((4, 256, 512), BF),
        pltpu.VMEM((1024, 512), BF),
        pltpu.VMEM((4, 256, 256), BF),
        pltpu.VMEM((3, 256, 1024), BF),
        pltpu.VMEM((8, 16), jnp.int32),
        pltpu.VMEM((4, 8, 128), F32),
        pltpu.VMEM((1024, 256), BF),
        pltpu.VMEM((1024, 256), BF),
        pltpu.VMEM((1024, 128), F32),
        pltpu.VMEM((1024, 128), F32),
        pltpu.VMEM((4, 128, 128), F32),
        pltpu.VMEM((4, 128, 128), BF),
        pltpu.VMEM((3, 128, 128), BF),
        pltpu.VMEM((256, 128), BF),
        pltpu.VMEM((8, 32, 128), BF),
        pltpu.VMEM((8, 64, 128), BF),
        pltpu.VMEM((7, 64, 128), BF),
        pltpu.VMEM((3, 64, 128), BF),
        pltpu.VMEM((1024, 512), BF),
        pltpu.SemaphoreType.REGULAR,
        dma((5,)),
        dma((3,)), dma((3,)), dma((24,)), dma((24,)), dma((6,)), dma((6,)),
        dma((3,)), dma((3,)), dma((7,)), dma((7,)), dma((7,)), dma((7,)),
        dma((2,)), dma((2,)), dma((7,)), dma((7,)), dma((3,)), dma((3,)),
        dma((4,)), dma((4,)),
    ]
    moment_next, update = pl.pallas_call(
        kernel,
        out_shape=(
            jax.ShapeDtypeStruct((1024, 512), BF),
            jax.ShapeDtypeStruct((1024, 512), BF),
        ),
        in_specs=[anywhere] * 5,
        out_specs=(pl.BlockSpec(memory_space=pltpu.VMEM),) * 2,
        scratch_shapes=scratch,
        compiler_params=pltpu.CompilerParams(
            collective_id=0, has_side_effects=True, vmem_limit_bytes=62 * 1024 * 1024
        ),
        name="step",
    )(
        activations, output_grads, momentum, picks,
        jnp.asarray(np.stack([high, low, high.T, low.T])),
    )
    return (moment_next[None], update.astype(F32))


def solution(mesh):
    return jax.shard_map(
        body,
        mesh=mesh,
        in_specs=(
            P(("replica", "fsdp"), None),
            P(("replica", "fsdp"), None),
            P("replica", "fsdp", None),
            P("replica", "fsdp", None),
        ),
        out_specs=(P("replica", "fsdp", None), P("fsdp", None)),
        check_vma=False,
    )
```

```python
import math

import jax
import jax.numpy as jnp
import numpy as np
from jax import lax
from jax.experimental import pallas as pl
from jax.experimental.pallas import tpu as pltpu
from jax.sharding import PartitionSpec as P

MESH = pl.DeviceIdType.MESH
F32 = jnp.float32
BF = jnp.bfloat16
SPAN = 64
NX, NY, NZ, NF = 8, 8, 3, 4
SLABS = 4
PIECES = 8


def tables():
    order = np.arange(SPAN)[:, None]
    place = np.arange(SPAN)[None, :]
    factor = np.where(order == 0, math.sqrt(1.0 / SPAN), math.sqrt(2.0 / SPAN))
    table = factor * np.cos(np.pi * (2 * place + 1) * order / (2 * SPAN))
    block = np.kron(np.eye(4), table).astype(np.float32)
    high = block.astype(jnp.bfloat16)
    low = (block - high.astype(np.float32)).astype(jnp.bfloat16)
    return high, low


def dot(a, b, ca=1, cb=0):
    return lax.dot_general(a, b, (((ca,), (cb,)), ((), ())), preferred_element_type=F32)


def split(a):
    high = a.astype(BF)
    return high, (a - high.astype(F32)).astype(BF)


def dot3(a, b, ca=1, cb=0):
    return dot(a[0], b[0], ca, cb) + dot(a[0], b[1], ca, cb) + dot(a[1], b[0], ca, cb)


def lanes_transform(value, table, cb):
    high, low = split(value)
    width = value.shape[1] // 256
    return jnp.concatenate(
        [
            dot3((high[:, 256 * t : 256 * t + 256], low[:, 256 * t : 256 * t + 256]), table, 1, cb)
            for t in range(width)
        ],
        axis=1,
    )


def iota(shape, dim):
    return lax.broadcasted_iota(jnp.int32, shape, dim)


def fold(value, span_col):
    lane = iota((value.shape[0], 128), 1)
    half = jnp.floor(span_col * 0.5)
    odd = span_col - 2.0 * half
    kept = jnp.zeros((value.shape[0], 128), F32)
    for s in range(4):
        kept = kept + jnp.where(half == float(s), value[:, 128 * s : 128 * s + 128], 0.0)
    kept = jnp.where((lane >> 6).astype(F32) == odd, kept, 0.0)
    return kept + pltpu.roll(kept, 64, 1)


def pack(rows):
    lane = iota((128, 128), 1)
    return jnp.where(lane < 64, rows[:128], rows[128:])


def kernel(
    x_hbm, g_hbm, mom_hbm, pk_hbm, tab_hbm,
    out_m, out_u,
    xv, g_all, mv, tab, xr, pk_own, pk_all, csh, csl, jrow, trow, upart, usend, urecv,
    sent, a2, dp, by, zb, fin, mout,
    gate, lsem, pk_s, pk_r, x_s, x_r, g_s, g_r, u_s, u_r, a_s, a_r, b_s, b_r,
    z_s, z_r, y_s, y_r, w_s, w_r, c_s, c_r,
):
    rep = lax.axis_index("replica")
    f = lax.axis_index("fsdp")
    m = lax.rem(rep, NX)
    row = rep - m
    y = lax.rem(lax.div(rep, NX), NY)
    zh = lax.div(rep, NX * NY)
    plane = lax.rem(rep, NX * NY)

    def line_peer(o):
        return (rep, lax.rem(f + o, NF))

    def row_peer(o):
        return (row + lax.rem(m + o, NX), f)

    def col_peer(o):
        return (zh * (NX * NY) + lax.rem(y + o, NY) * NX + m, f)

    def hi_peer(o):
        return (lax.rem(zh + o, NZ) * (NX * NY) + plane, f)

    loads = [
        pltpu.make_async_copy(x_hbm, xv, lsem.at[0]),
        pltpu.make_async_copy(g_hbm, g_all.at[f], lsem.at[1]),
        pltpu.make_async_copy(mom_hbm.at[0], mv, lsem.at[2]),
        pltpu.make_async_copy(tab_hbm, tab, lsem.at[3]),
        pltpu.make_async_copy(pk_hbm, pk_own, lsem.at[4]),
    ]
    for copy in loads:
        copy.start()

    barrier = pltpu.get_barrier_semaphore()
    core = lax.rem(m, 2)
    other = (rep + 1 - 2 * core, f)

    def enter(there):
        pl.semaphore_signal(barrier, inc=1, device_id=there, device_id_type=MESH)

    for o in range(1, NF):
        enter((rep - core, lax.rem(f + o, NF)))
    for o in range(2, NX, 2):
        enter((row + lax.rem(m - core + o, NX), f))
    for o in range(1, NY):
        enter((zh * (NX * NY) + lax.rem(y + o, NY) * NX + m - core, f))
    for o in range(1, NZ):
        enter((lax.rem(zh + o, NZ) * (NX * NY) + plane - core + 1, f))

    @pl.when(core == 1)
    def _():
        enter(other)

    for copy in (loads[4],):
        copy.wait()
    pk_all[f] = jnp.zeros((8, 128), F32)
    pk_all[f, :, :16] = pk_own[...].astype(F32)

    @pl.when(core == 0)
    def _():
        pl.semaphore_wait(barrier, 2 * (NF - 1) + (NX - 1) + 2 * (NY - 1))
        pl.semaphore_signal(gate, inc=1, device_id=other, device_id_type=MESH)

    @pl.when(core == 1)
    def _():
        pl.semaphore_wait(gate, 1)

    sends = []

    def remote(src, dst, ssem, rsem, peer):
        copy = pltpu.make_async_remote_copy(
            src_ref=src, dst_ref=dst, send_sem=ssem, recv_sem=rsem,
            device_id=peer, device_id_type=MESH,
        )
        copy.start()
        sends.append(copy)
        return copy

    pk_copies = [
        remote(pk_all.at[f], pk_all.at[f], pk_s.at[o - 1], pk_r.at[o - 1], line_peer(o))
        for o in range(1, NF)
    ]

    x_copies = [[] for _ in range(PIECES)]

    def send_x(pieces, offsets=None):
        for piece in pieces:
            for step in range(NF - 1) if offsets is None else offsets:
                o = step
                if offsets is None:
                    target = step + 1 - lax.div(f + NF - 1 - step, NF)
                    o = lax.rem(target - f + NF, NF)
                peer = lax.rem(f + o, NF)
                cols = pl.ds(pl.multiple_of(peer * 1024 + piece * 128, 128), 128)
                k = piece * 3 + o - 1
                x_copies[piece].append(
                    remote(
                        x_hbm.at[:, cols], xr.at[o - 1, :, pl.ds(piece * 128, 128)],
                        x_s.at[k], x_r.at[k], line_peer(o),
                    )
                )

    def relay(hop, direction):
        step = 1 - 2 * direction
        source = f - step * hop
        present = (source >= 0) & (source < NF)
        onward = present & (f + step >= 0) & (f + step < NF)
        slot = lax.rem(source + NF, NF)
        copy = pltpu.make_async_remote_copy(
            src_ref=g_all.at[slot], dst_ref=g_all.at[slot],
            send_sem=g_s.at[direction * 3 + lax.rem(hop, 3)], recv_sem=g_r.at[direction * 3 + hop],
            device_id=(rep, lax.rem(f + step + NF, NF)), device_id_type=MESH,
        )
        return present, onward, copy

    def send_g(hop):
        for direction in range(2):
            _, onward, copy = relay(hop, direction)

            @pl.when(onward)
            def _():
                copy.start()

    def wait_g(hop):
        for direction in range(2):
            step = 1 - 2 * direction
            source = f - step * hop
            slot = lax.rem(source + NF, NF)

            @pl.when((source >= 0) & (source < NF))
            def _():
                pltpu.make_async_remote_copy(
                    src_ref=g_all.at[slot], dst_ref=g_all.at[slot],
                    send_sem=g_s.at[direction * 3], recv_sem=g_r.at[direction * 3 + hop - 1],
                    device_id=(rep, lax.rem(f + step + NF, NF)), device_id_type=MESH,
                ).wait_recv()


    for copy in (loads[1], loads[3]):
        copy.wait()
    send_g(0)
    send_x([0])
    table = (tab[0], tab[1])
    gv = g_all[f]
    gc = split(
        jnp.concatenate(
            [
                dot(gv[:, 256 * t : 256 * t + 256], table[0], 1, 1)
                + dot(gv[:, 256 * t : 256 * t + 256], table[1], 1, 1)
                for t in range(2)
            ],
            axis=1,
        )
    )

    rows = iota((256, 128), 0)
    lane = iota((256, 128), 1)
    pick_lane = lane == (rows >> 4)
    spread = (iota((256, 8), 1) == ((iota((256, 8), 0) >> 1) & 7)).astype(BF)
    odd_row = (rows & 1).astype(F32)
    lane2 = iota((256, 256), 1).astype(F32)
    shift = (((iota((256, 1), 0) >> 4) & 3) * 64).astype(F32)

    def chosen_rows(fi):
        picks = dot(spread, pk_all[fi].astype(BF))
        number = jnp.sum(jnp.where(pick_lane, picks, 0.0), axis=1, keepdims=True)
        col = jnp.floor(number * (1.0 / 32.0))
        coeff_row = 2.0 * (number - 32.0 * col) + odd_row[:, :1]
        onehot = jnp.where(lane2 == coeff_row + shift, 1.0, 0.0).astype(BF)
        return dot(onehot, table[0]).astype(BF), dot(onehot, table[1]).astype(BF), col, coeff_row

    def times(high, low, other_side, cb):
        both = dot(jnp.concatenate([high, low], axis=0), other_side, 1, cb)
        return both[:64] + both[64:]

    def contribution(fi, high, low, col_b):
        parts = []
        for s in range(SLABS):
            cols = pl.ds(pl.multiple_of(fi * 1024 + s * 256, 256), 256)
            at = slice(64 * s, 64 * s + 64)
            parts.append(times(high[at], low[at], xv[:, cols], 1))
        return pack(fold(dot3(split(jnp.concatenate(parts, axis=0)), gc), col_b))

    own_high, own_low, own_col, own_row = chosen_rows(f)
    csh[...] = own_high
    csl[...] = own_low
    col_b = jnp.broadcast_to(own_col, (256, 128))
    jrow[...] = col_b
    trow[...] = jnp.broadcast_to(own_row + 64.0 * jnp.floor(own_col * 0.5), (256, 128))
    loads[2].wait()
    parts = []
    for s in range(SLABS):
        at = slice(64 * s, 64 * s + 64)
        parts.append(times(own_high[at], own_low[at], mv[256 * s : 256 * s + 256, :], 0))
    upart[...] = 0.9 * pack(fold(lanes_transform(jnp.concatenate(parts, axis=0), table, 1), col_b))
    loads[0].wait()
    u_copies = []
    for o in range(1, NF):
        pk_copies[NF - o - 1].wait_recv()
        fi = lax.rem(f + o, NF)
        high, low, col, _ = chosen_rows(fi)
        usend[o - 1] = contribution(fi, high, low, jnp.broadcast_to(col, (256, 128))).astype(BF)
        u_copies.append(
            remote(usend.at[o - 1], urecv.at[o - 1], u_s.at[o - 1], u_r.at[o - 1], line_peer(o))
        )
    wait_g(1)
    send_g(1)
    send_x([1])
    col_b = jrow[...]
    packed = upart[...] + contribution(f, csh[...], csl[...], col_b)
    for copy in u_copies:
        copy.wait_recv()
    for o in range(3):
        packed = packed + urecv[o].astype(F32)
    packed = jnp.concatenate([packed, pltpu.roll(packed, 64, 1)], axis=0)
    col_odd = col_b - 2.0 * jnp.floor(col_b * 0.5)
    tile = jnp.where(lane < 64, packed, jnp.where(lane < 96, trow[...], col_odd))
    sent[...] = tile.astype(BF)

    a_copies = []
    for o in range(1, NX):
        there = pl.ds(pl.multiple_of(lax.rem(m + o, NX) * 32, 32), 32)
        a_copies.append(
            remote(sent.at[there, :], a2.at[o - 1], a_s.at[o - 1], a_r.at[o - 1], row_peer(o))
        )
    a2[NX - 1] = sent[pl.ds(pl.multiple_of(m * 32, 32), 32), :]
    for copy in a_copies:
        copy.wait_recv()
    lane1 = iota((128, 128), 1)
    lane256 = iota((128, 256), 1).astype(F32)
    for u in range(2):
        got = jnp.concatenate(
            [a2[o, 16 * u : 16 * u + 16, :] for o in range(NX)], axis=0
        ).astype(F32)
        value = jnp.where(lane1 < 64, got, 0.0)
        value = value + pltpu.roll(value, 64, 1)
        value = jnp.where((lane1 >> 6).astype(F32) == got[:, 96:97], value, 0.0)
        onehot = jnp.where(lane256 == got[:, 64:65], 1.0, 0.0)
        dense = dot(onehot.astype(BF), value.astype(BF), 0, 0).astype(BF)
        for s in range(4):
            dp[4 * u + s] = dense[64 * s : 64 * s + 64]
    b_copies = [
        remote(
            dp.at[lax.rem(y + o, NY)], by.at[o - 1], b_s.at[o - 1], b_r.at[o - 1], col_peer(o)
        )
        for o in range(1, NY)
    ]
    plane_sum = dp[y].astype(F32)
    for copy in b_copies:
        copy.wait_recv()
    for o in range(NY - 1):
        plane_sum = plane_sum + by[o].astype(F32)
    zb[zh] = plane_sum.astype(BF)

    @pl.when(core == 1)
    def _():
        pl.semaphore_wait(barrier, 2 * (NZ - 1))
        pl.semaphore_signal(gate, inc=1, device_id=other, device_id_type=MESH)

    @pl.when(core == 0)
    def _():
        pl.semaphore_wait(gate, 1)

    z_copies = [
        remote(zb.at[zh], zb.at[zh], z_s.at[o - 1], z_r.at[o - 1], hi_peer(o))
        for o in range(1, NZ)
    ]
    send_x([2])
    wait_g(2)
    send_g(2)
    send_x(range(3, PIECES))
    for copy in z_copies:
        copy.wait_recv()
    total = zb[0].astype(F32) + zb[1].astype(F32) + zb[2].astype(F32)
    left = dot3((tab[2, :64, :64], tab[3, :64, :64]), split(total))
    piece = dot3(split(left), (tab[0, :128, :128], tab[1, :128, :128]))
    piece_rows = pl.ds(pl.multiple_of(m * 128 + lax.div(y, 4) * 64, 64), 64)
    piece_cols = pl.ds(pl.multiple_of(lax.rem(y, 4) * 128, 128), 128)
    fin[piece_rows, piece_cols] = piece.astype(BF)
    y_copies = [
        remote(
            fin.at[piece_rows, piece_cols], fin.at[piece_rows, piece_cols],
            y_s.at[o - 1], y_r.at[o - 1], col_peer(o),
        )
        for o in range(1, NY)
    ]
    lane512 = (iota((64, 512), 1) >> 6).astype(F32)

    m_out = []

    def slab(first, count):
        for piece in range(first, first + count):
            for copy in x_copies[piece]:
                copy.wait_recv()
        size = 128 * count
        at = slice(128 * first, 128 * first + size)
        picked = slice(32 * first, 32 * first + 32 * count)
        part = slice(128 * (first % 2), 128 * (first % 2) + size)
        cols = pl.ds(pl.multiple_of(f * 1024 + 128 * first, 128), size)
        moment = 0.9 * mv[at, :].astype(F32)
        moment = moment + dot(xv[:, cols], g_all[f], 0, 0)
        for o in range(1, NF):
            source = lax.rem(f + NF - o, NF)
            moment = moment + dot(xr[o - 1, :, at], g_all[source], 0, 0)
        cs = (csh[picked, part], csl[picked, part])
        coeff = lanes_transform(dot3(cs, split(moment)), table, 1)
        coeff = jnp.where(lane512[: 32 * count] == jrow[picked, :1], coeff, 0.0)
        chosen = dot3(cs, split(lanes_transform(coeff, table, 0)), 0, 0)
        mout[at, :] = (moment - chosen).astype(BF)
        copy = pltpu.make_async_copy(mout.at[at, :], out_m.at[at, :], lsem.at[5 + len(m_out)])
        copy.start()
        m_out.append(copy)

    for copy in y_copies:
        copy.wait_recv()
    band = pl.ds(pl.multiple_of(m * 128, 128), 128)
    w_copies = [
        remote(fin.at[band, :], fin.at[band, :], w_s.at[o - 1], w_r.at[o - 1], row_peer(2 * o))
        for o in range(1, 4)
    ]
    c_copies = [remote(fin.at[band, :], fin.at[band, :], c_s.at[0], c_r.at[0], other)]
    wait_g(3)
    slab(0, 2)
    for o in range(1, 4):
        w_copies[o - 1].wait_recv()
        there = pl.ds(pl.multiple_of(lax.rem(m + NX - 2 * o, NX) * 128, 128), 128)
        c_copies.append(remote(fin.at[there, :], fin.at[there, :], c_s.at[o], c_r.at[o], other))
    slab(2, 2)
    slab(4, 2)
    for copy in c_copies:
        copy.wait_recv()
    u_out = pltpu.make_async_copy(fin, out_u, lsem.at[0])
    u_out.start()
    slab(6, 1)
    slab(7, 1)

    for copy in sends:
        copy.wait_send()
    for hop in range(3):
        for direction in range(2):
            _, onward, copy = relay(hop, direction)

            @pl.when(onward)
            def _():
                copy.wait_send()

    u_out.wait()
    for copy in m_out:
        copy.wait()


def body(activations, output_grads, momentum, chosen_blocks):
    high, low = tables()
    picks = chosen_blocks[0].T
    dma = pltpu.SemaphoreType.DMA
    anywhere = pl.BlockSpec(memory_space=pl.ANY)
    scratch = [
        pltpu.VMEM((256, 4096), BF),
        pltpu.VMEM((4, 256, 512), BF),
        pltpu.VMEM((1024, 512), BF),
        pltpu.VMEM((4, 256, 256), BF),
        pltpu.VMEM((3, 256, 1024), BF),
        pltpu.VMEM((8, 16), jnp.int32),
        pltpu.VMEM((4, 8, 128), F32),
        pltpu.VMEM((256, 256), BF),
        pltpu.VMEM((256, 256), BF),
        pltpu.VMEM((256, 128), F32),
        pltpu.VMEM((256, 128), F32),
        pltpu.VMEM((128, 128), F32),
        pltpu.VMEM((3, 128, 128), BF),
        pltpu.VMEM((3, 128, 128), BF),
        pltpu.VMEM((256, 128), BF),
        pltpu.VMEM((8, 32, 128), BF),
        pltpu.VMEM((8, 64, 128), BF),
        pltpu.VMEM((7, 64, 128), BF),
        pltpu.VMEM((3, 64, 128), BF),
        pltpu.VMEM((1024, 512), BF),
        pltpu.VMEM((1024, 512), BF),
        pltpu.SemaphoreType.REGULAR,
        dma((10,)),
        dma((3,)), dma((3,)), dma((24,)), dma((24,)), dma((6,)), dma((6,)),
        dma((3,)), dma((3,)), dma((7,)), dma((7,)), dma((7,)), dma((7,)),
        dma((2,)), dma((2,)), dma((7,)), dma((7,)), dma((3,)), dma((3,)),
        dma((4,)), dma((4,)),
    ]
    moment_next, update = pl.pallas_call(
        kernel,
        out_shape=(
            jax.ShapeDtypeStruct((1024, 512), BF),
            jax.ShapeDtypeStruct((1024, 512), BF),
        ),
        in_specs=[anywhere] * 5,
        out_specs=(anywhere, anywhere),
        scratch_shapes=scratch,
        compiler_params=pltpu.CompilerParams(
            collective_id=0, has_side_effects=True, vmem_limit_bytes=62 * 1024 * 1024
        ),
        name="step",
    )(
        activations, output_grads, momentum, picks,
        jnp.asarray(np.stack([high, low, high.T, low.T])),
    )
    return (moment_next[None], update.astype(F32))


def solution(mesh):
    return jax.shard_map(
        body,
        mesh=mesh,
        in_specs=(
            P(("replica", "fsdp"), None),
            P(("replica", "fsdp"), None),
            P("replica", "fsdp", None),
            P("replica", "fsdp", None),
        ),
        out_specs=(P("replica", "fsdp", None), P("fsdp", None)),
        check_vma=False,
    )
```

```python
import math

import jax
import jax.numpy as jnp
import numpy as np
from jax import lax
from jax.experimental import pallas as pl
from jax.experimental.pallas import tpu as pltpu
from jax.sharding import PartitionSpec as P

MESH = pl.DeviceIdType.MESH
F32 = jnp.float32
BF = jnp.bfloat16
SPAN = 64
NX, NY, NZ, NF = 8, 8, 3, 4
SLABS = 4
PIECES = 8


def tables():
    order = np.arange(SPAN)[:, None]
    place = np.arange(SPAN)[None, :]
    factor = np.where(order == 0, math.sqrt(1.0 / SPAN), math.sqrt(2.0 / SPAN))
    table = factor * np.cos(np.pi * (2 * place + 1) * order / (2 * SPAN))
    block = np.kron(np.eye(4), table).astype(np.float32)
    high = block.astype(jnp.bfloat16)
    low = (block - high.astype(np.float32)).astype(jnp.bfloat16)
    return high, low


def dot(a, b, ca=1, cb=0):
    return lax.dot_general(a, b, (((ca,), (cb,)), ((), ())), preferred_element_type=F32)


def split(a):
    high = a.astype(BF)
    return high, (a - high.astype(F32)).astype(BF)


def dot3(a, b, ca=1, cb=0):
    return dot(a[0], b[0], ca, cb) + dot(a[0], b[1], ca, cb) + dot(a[1], b[0], ca, cb)


def lanes_transform(value, table, cb):
    high, low = split(value)
    width = value.shape[1] // 256
    return jnp.concatenate(
        [
            dot3((high[:, 256 * t : 256 * t + 256], low[:, 256 * t : 256 * t + 256]), table, 1, cb)
            for t in range(width)
        ],
        axis=1,
    )


def iota(shape, dim):
    return lax.broadcasted_iota(jnp.int32, shape, dim)


def fold(value, span_col):
    lane = iota((value.shape[0], 128), 1)
    half = jnp.floor(span_col * 0.5)
    odd = span_col - 2.0 * half
    kept = jnp.zeros((value.shape[0], 128), F32)
    for s in range(4):
        kept = kept + jnp.where(half == float(s), value[:, 128 * s : 128 * s + 128], 0.0)
    kept = jnp.where((lane >> 6).astype(F32) == odd, kept, 0.0)
    return kept + pltpu.roll(kept, 64, 1)


def pack(rows):
    lane = iota((128, 128), 1)
    return jnp.where(lane < 64, rows[:128], rows[128:])


def kernel(
    x_hbm, g_hbm, mom_hbm, pk_hbm, tab_hbm,
    out_m, out_u,
    xv, g_all, mv, tab, xr, pk_own, pk_all, csh, csl, jrow, trow, upart, usend, urecv,
    sent, a2, dp, by, zb, fin, mout,
    gate, lsem, pk_s, pk_r, x_s, x_r, g_s, g_r, u_s, u_r, a_s, a_r, b_s, b_r,
    z_s, z_r, y_s, y_r, w_s, w_r, c_s, c_r,
):
    rep = lax.axis_index("replica")
    f = lax.axis_index("fsdp")
    m = lax.rem(rep, NX)
    row = rep - m
    y = lax.rem(lax.div(rep, NX), NY)
    zh = lax.div(rep, NX * NY)
    plane = lax.rem(rep, NX * NY)

    def line_peer(o):
        return (rep, lax.rem(f + o, NF))

    def row_peer(o):
        return (row + lax.rem(m + o, NX), f)

    def col_peer(o):
        return (zh * (NX * NY) + lax.rem(y + o, NY) * NX + m, f)

    def hi_peer(o):
        return (lax.rem(zh + o, NZ) * (NX * NY) + plane, f)

    loads = [
        pltpu.make_async_copy(x_hbm, xv, lsem.at[0]),
        pltpu.make_async_copy(g_hbm, g_all.at[f], lsem.at[1]),
        pltpu.make_async_copy(mom_hbm.at[0], mv, lsem.at[2]),
        pltpu.make_async_copy(tab_hbm, tab, lsem.at[3]),
        pltpu.make_async_copy(pk_hbm, pk_own, lsem.at[4]),
    ]
    for copy in loads:
        copy.start()

    barrier = pltpu.get_barrier_semaphore()
    core = lax.rem(m, 2)
    other = (rep + 1 - 2 * core, f)

    def enter(there):
        pl.semaphore_signal(barrier, inc=1, device_id=there, device_id_type=MESH)

    for o in range(1, NF):
        enter((rep - core, lax.rem(f + o, NF)))
    for o in range(2, NX, 2):
        enter((row + lax.rem(m - core + o, NX), f))
    for o in range(1, NY):
        enter((zh * (NX * NY) + lax.rem(y + o, NY) * NX + m - core, f))
    for o in range(1, NZ):
        enter((lax.rem(zh + o, NZ) * (NX * NY) + plane - core + 1, f))

    @pl.when(core == 1)
    def _():
        enter(other)

    for copy in (loads[4],):
        copy.wait()
    pk_all[f] = jnp.zeros((8, 128), F32)
    pk_all[f, :, :16] = pk_own[...].astype(F32)

    @pl.when(core == 0)
    def _():
        pl.semaphore_wait(barrier, 2 * (NF - 1) + (NX - 1) + 2 * (NY - 1))
        pl.semaphore_signal(gate, inc=1, device_id=other, device_id_type=MESH)

    @pl.when(core == 1)
    def _():
        pl.semaphore_wait(gate, 1)

    sends = []

    def remote(src, dst, ssem, rsem, peer):
        copy = pltpu.make_async_remote_copy(
            src_ref=src, dst_ref=dst, send_sem=ssem, recv_sem=rsem,
            device_id=peer, device_id_type=MESH,
        )
        copy.start()
        sends.append(copy)
        return copy

    pk_copies = [
        remote(pk_all.at[f], pk_all.at[f], pk_s.at[o - 1], pk_r.at[o - 1], line_peer(o))
        for o in range(1, NF)
    ]

    x_copies = [[] for _ in range(PIECES)]

    def send_x(pieces, offsets=None):
        for piece in pieces:
            for step in range(NF - 1) if offsets is None else offsets:
                o = step
                if offsets is None:
                    target = NF - 1 - step - lax.div(f + 1 + step, NF)
                    o = lax.rem(target - f + NF, NF)
                peer = lax.rem(f + o, NF)
                cols = pl.ds(pl.multiple_of(peer * 1024 + piece * 128, 128), 128)
                k = piece * 3 + o - 1
                x_copies[piece].append(
                    remote(
                        x_hbm.at[:, cols], xr.at[o - 1, :, pl.ds(piece * 128, 128)],
                        x_s.at[k], x_r.at[k], line_peer(o),
                    )
                )

    def relay(hop, direction):
        step = 1 - 2 * direction
        source = f - step * hop
        present = (source >= 0) & (source < NF)
        onward = present & (f + step >= 0) & (f + step < NF)
        slot = lax.rem(source + NF, NF)
        copy = pltpu.make_async_remote_copy(
            src_ref=g_all.at[slot], dst_ref=g_all.at[slot],
            send_sem=g_s.at[direction * 3 + lax.rem(hop, 3)], recv_sem=g_r.at[direction * 3 + hop],
            device_id=(rep, lax.rem(f + step + NF, NF)), device_id_type=MESH,
        )
        return present, onward, copy

    def send_g(hop):
        for direction in range(2):
            _, onward, copy = relay(hop, direction)

            @pl.when(onward)
            def _():
                copy.start()

    def wait_g(hop):
        for direction in range(2):
            step = 1 - 2 * direction
            source = f - step * hop
            slot = lax.rem(source + NF, NF)

            @pl.when((source >= 0) & (source < NF))
            def _():
                pltpu.make_async_remote_copy(
                    src_ref=g_all.at[slot], dst_ref=g_all.at[slot],
                    send_sem=g_s.at[direction * 3], recv_sem=g_r.at[direction * 3 + hop - 1],
                    device_id=(rep, lax.rem(f + step + NF, NF)), device_id_type=MESH,
                ).wait_recv()


    for copy in (loads[1], loads[3]):
        copy.wait()
    send_g(0)
    send_x([0])
    table = (tab[0], tab[1])
    gv = g_all[f]
    gc = split(
        jnp.concatenate(
            [
                dot(gv[:, 256 * t : 256 * t + 256], table[0], 1, 1)
                + dot(gv[:, 256 * t : 256 * t + 256], table[1], 1, 1)
                for t in range(2)
            ],
            axis=1,
        )
    )

    rows = iota((256, 128), 0)
    lane = iota((256, 128), 1)
    pick_lane = lane == (rows >> 4)
    spread = (iota((256, 8), 1) == ((iota((256, 8), 0) >> 1) & 7)).astype(BF)
    odd_row = (rows & 1).astype(F32)
    lane2 = iota((256, 256), 1).astype(F32)
    shift = (((iota((256, 1), 0) >> 4) & 3) * 64).astype(F32)

    def chosen_rows(fi):
        picks = dot(spread, pk_all[fi].astype(BF))
        number = jnp.sum(jnp.where(pick_lane, picks, 0.0), axis=1, keepdims=True)
        col = jnp.floor(number * (1.0 / 32.0))
        coeff_row = 2.0 * (number - 32.0 * col) + odd_row[:, :1]
        onehot = jnp.where(lane2 == coeff_row + shift, 1.0, 0.0).astype(BF)
        return dot(onehot, table[0]).astype(BF), dot(onehot, table[1]).astype(BF), col, coeff_row

    def times(high, low, other_side, cb):
        both = dot(jnp.concatenate([high, low], axis=0), other_side, 1, cb)
        return both[:64] + both[64:]

    def contribution(fi, high, low, col_b):
        parts = []
        for s in range(SLABS):
            cols = pl.ds(pl.multiple_of(fi * 1024 + s * 256, 256), 256)
            at = slice(64 * s, 64 * s + 64)
            parts.append(times(high[at], low[at], xv[:, cols], 1))
        return pack(fold(dot3(split(jnp.concatenate(parts, axis=0)), gc), col_b))

    own_high, own_low, own_col, own_row = chosen_rows(f)
    csh[...] = own_high
    csl[...] = own_low
    col_b = jnp.broadcast_to(own_col, (256, 128))
    jrow[...] = col_b
    trow[...] = jnp.broadcast_to(own_row + 64.0 * jnp.floor(own_col * 0.5), (256, 128))
    loads[2].wait()
    parts = []
    for s in range(SLABS):
        at = slice(64 * s, 64 * s + 64)
        parts.append(times(own_high[at], own_low[at], mv[256 * s : 256 * s + 256, :], 0))
    upart[...] = 0.9 * pack(fold(lanes_transform(jnp.concatenate(parts, axis=0), table, 1), col_b))
    loads[0].wait()
    u_copies = []
    for o in range(1, NF):
        pk_copies[NF - o - 1].wait_recv()
        fi = lax.rem(f + o, NF)
        high, low, col, _ = chosen_rows(fi)
        usend[o - 1] = contribution(fi, high, low, jnp.broadcast_to(col, (256, 128))).astype(BF)
        u_copies.append(
            remote(usend.at[o - 1], urecv.at[o - 1], u_s.at[o - 1], u_r.at[o - 1], line_peer(o))
        )
    wait_g(1)
    send_g(1)
    send_x([1])
    send_x([2], (2,))
    col_b = jrow[...]
    packed = upart[...] + contribution(f, csh[...], csl[...], col_b)
    for copy in u_copies:
        copy.wait_recv()
    for o in range(3):
        packed = packed + urecv[o].astype(F32)
    packed = jnp.concatenate([packed, pltpu.roll(packed, 64, 1)], axis=0)
    col_odd = col_b - 2.0 * jnp.floor(col_b * 0.5)
    tile = jnp.where(lane < 64, packed, jnp.where(lane < 96, trow[...], col_odd))
    sent[...] = tile.astype(BF)

    a_copies = []
    for o in range(1, NX):
        there = pl.ds(pl.multiple_of(lax.rem(m + o, NX) * 32, 32), 32)
        a_copies.append(
            remote(sent.at[there, :], a2.at[o - 1], a_s.at[o - 1], a_r.at[o - 1], row_peer(o))
        )
    a2[NX - 1] = sent[pl.ds(pl.multiple_of(m * 32, 32), 32), :]
    for copy in a_copies:
        copy.wait_recv()
    lane1 = iota((128, 128), 1)
    lane256 = iota((128, 256), 1).astype(F32)
    for u in range(2):
        got = jnp.concatenate(
            [a2[o, 16 * u : 16 * u + 16, :] for o in range(NX)], axis=0
        ).astype(F32)
        value = jnp.where(lane1 < 64, got, 0.0)
        value = value + pltpu.roll(value, 64, 1)
        value = jnp.where((lane1 >> 6).astype(F32) == got[:, 96:97], value, 0.0)
        onehot = jnp.where(lane256 == got[:, 64:65], 1.0, 0.0)
        dense = dot(onehot.astype(BF), value.astype(BF), 0, 0).astype(BF)
        for s in range(4):
            dp[4 * u + s] = dense[64 * s : 64 * s + 64]
    b_copies = [
        remote(
            dp.at[lax.rem(y + o, NY)], by.at[o - 1], b_s.at[o - 1], b_r.at[o - 1], col_peer(o)
        )
        for o in range(1, NY)
    ]
    plane_sum = dp[y].astype(F32)
    for copy in b_copies:
        copy.wait_recv()
    for o in range(NY - 1):
        plane_sum = plane_sum + by[o].astype(F32)
    zb[zh] = plane_sum.astype(BF)

    @pl.when(core == 1)
    def _():
        pl.semaphore_wait(barrier, 2 * (NZ - 1))
        pl.semaphore_signal(gate, inc=1, device_id=other, device_id_type=MESH)

    @pl.when(core == 0)
    def _():
        pl.semaphore_wait(gate, 1)

    z_copies = [
        remote(zb.at[zh], zb.at[zh], z_s.at[o - 1], z_r.at[o - 1], hi_peer(o))
        for o in range(1, NZ)
    ]
    send_x([2], (3, 1))
    wait_g(2)
    send_g(2)
    send_x(range(3, PIECES))
    for copy in z_copies:
        copy.wait_recv()
    total = zb[0].astype(F32) + zb[1].astype(F32) + zb[2].astype(F32)
    left = dot3((tab[2, :64, :64], tab[3, :64, :64]), split(total))
    piece = dot3(split(left), (tab[0, :128, :128], tab[1, :128, :128]))
    piece_rows = pl.ds(pl.multiple_of(m * 128 + lax.div(y, 4) * 64, 64), 64)
    piece_cols = pl.ds(pl.multiple_of(lax.rem(y, 4) * 128, 128), 128)
    fin[piece_rows, piece_cols] = piece.astype(BF)
    y_copies = [
        remote(
            fin.at[piece_rows, piece_cols], fin.at[piece_rows, piece_cols],
            y_s.at[o - 1], y_r.at[o - 1], col_peer(o),
        )
        for o in range(1, NY)
    ]
    lane512 = (iota((64, 512), 1) >> 6).astype(F32)

    m_out = []

    def slab(first, count):
        for piece in range(first, first + count):
            for copy in x_copies[piece]:
                copy.wait_recv()
        size = 128 * count
        at = slice(128 * first, 128 * first + size)
        picked = slice(32 * first, 32 * first + 32 * count)
        part = slice(128 * (first % 2), 128 * (first % 2) + size)
        cols = pl.ds(pl.multiple_of(f * 1024 + 128 * first, 128), size)
        moment = 0.9 * mv[at, :].astype(F32)
        moment = moment + dot(xv[:, cols], g_all[f], 0, 0)
        for o in range(1, NF):
            source = lax.rem(f + NF - o, NF)
            moment = moment + dot(xr[o - 1, :, at], g_all[source], 0, 0)
        cs = (csh[picked, part], csl[picked, part])
        coeff = lanes_transform(dot3(cs, split(moment)), table, 1)
        coeff = jnp.where(lane512[: 32 * count] == jrow[picked, :1], coeff, 0.0)
        chosen = dot3(cs, split(lanes_transform(coeff, table, 0)), 0, 0)
        mout[at, :] = (moment - chosen).astype(BF)
        copy = pltpu.make_async_copy(mout.at[at, :], out_m.at[at, :], lsem.at[5 + len(m_out)])
        copy.start()
        m_out.append(copy)

    for copy in y_copies:
        copy.wait_recv()
    band = pl.ds(pl.multiple_of(m * 128, 128), 128)
    w_copies = [
        remote(fin.at[band, :], fin.at[band, :], w_s.at[o - 1], w_r.at[o - 1], row_peer(2 * o))
        for o in range(1, 4)
    ]
    c_copies = [remote(fin.at[band, :], fin.at[band, :], c_s.at[0], c_r.at[0], other)]
    wait_g(3)
    slab(0, 2)
    for o in range(1, 4):
        w_copies[o - 1].wait_recv()
        there = pl.ds(pl.multiple_of(lax.rem(m + NX - 2 * o, NX) * 128, 128), 128)
        c_copies.append(remote(fin.at[there, :], fin.at[there, :], c_s.at[o], c_r.at[o], other))
    slab(2, 2)
    slab(4, 2)
    for copy in c_copies:
        copy.wait_recv()
    u_out = pltpu.make_async_copy(fin, out_u, lsem.at[0])
    u_out.start()
    slab(6, 1)
    slab(7, 1)

    for copy in sends:
        copy.wait_send()
    for hop in range(3):
        for direction in range(2):
            _, onward, copy = relay(hop, direction)

            @pl.when(onward)
            def _():
                copy.wait_send()

    u_out.wait()
    for copy in m_out:
        copy.wait()


def body(activations, output_grads, momentum, chosen_blocks):
    high, low = tables()
    picks = chosen_blocks[0].T
    dma = pltpu.SemaphoreType.DMA
    anywhere = pl.BlockSpec(memory_space=pl.ANY)
    scratch = [
        pltpu.VMEM((256, 4096), BF),
        pltpu.VMEM((4, 256, 512), BF),
        pltpu.VMEM((1024, 512), BF),
        pltpu.VMEM((4, 256, 256), BF),
        pltpu.VMEM((3, 256, 1024), BF),
        pltpu.VMEM((8, 16), jnp.int32),
        pltpu.VMEM((4, 8, 128), F32),
        pltpu.VMEM((256, 256), BF),
        pltpu.VMEM((256, 256), BF),
        pltpu.VMEM((256, 128), F32),
        pltpu.VMEM((256, 128), F32),
        pltpu.VMEM((128, 128), F32),
        pltpu.VMEM((3, 128, 128), BF),
        pltpu.VMEM((3, 128, 128), BF),
        pltpu.VMEM((256, 128), BF),
        pltpu.VMEM((8, 32, 128), BF),
        pltpu.VMEM((8, 64, 128), BF),
        pltpu.VMEM((7, 64, 128), BF),
        pltpu.VMEM((3, 64, 128), BF),
        pltpu.VMEM((1024, 512), BF),
        pltpu.VMEM((1024, 512), BF),
        pltpu.SemaphoreType.REGULAR,
        dma((10,)),
        dma((3,)), dma((3,)), dma((24,)), dma((24,)), dma((6,)), dma((6,)),
        dma((3,)), dma((3,)), dma((7,)), dma((7,)), dma((7,)), dma((7,)),
        dma((2,)), dma((2,)), dma((7,)), dma((7,)), dma((3,)), dma((3,)),
        dma((4,)), dma((4,)),
    ]
    moment_next, update = pl.pallas_call(
        kernel,
        out_shape=(
            jax.ShapeDtypeStruct((1024, 512), BF),
            jax.ShapeDtypeStruct((1024, 512), BF),
        ),
        in_specs=[anywhere] * 5,
        out_specs=(anywhere, anywhere),
        scratch_shapes=scratch,
        compiler_params=pltpu.CompilerParams(
            collective_id=0, has_side_effects=True, vmem_limit_bytes=62 * 1024 * 1024
        ),
        name="step",
    )(
        activations, output_grads, momentum, picks,
        jnp.asarray(np.stack([high, low, high.T, low.T])),
    )
    return (moment_next[None], update.astype(F32))


def solution(mesh):
    return jax.shard_map(
        body,
        mesh=mesh,
        in_specs=(
            P(("replica", "fsdp"), None),
            P(("replica", "fsdp"), None),
            P("replica", "fsdp", None),
            P("replica", "fsdp", None),
        ),
        out_specs=(P("replica", "fsdp", None), P("fsdp", None)),
        check_vma=False,
    )
```
